512 devices in a mesh: wide: 64 (over z_lo, y, x), narrow: 8 (over z_hi, core).
Axes of the slice: x: 4, y: 8, z: 8 (z_hi: 4, z_lo: 2; z = z_hi * 2 + z_lo), core: 2. Of those that a mesh axis runs over, the one named last changes fastest.
Arguments:
- tokens: bfloat16 [4096, 2048], P('wide'), may hold values from -6 to 6
- routes: int32 [4096, 6], P('wide'), may hold values from 0 to 63, all different within a row; in each aligned block of 64 rows (0 to 63, 64 to 127, ...) at most 11 rows name the same one
- route_weight: float32 [4096, 6], P('wide'), may hold values from 0.1 to 0.8
- w_gate: bfloat16 [64, 1408, 2048], P('wide', None, 'narrow'), may hold values from -0.1875 to 0.1875
- w_up: bfloat16 [64, 1408, 2048], P('wide', None, 'narrow'), may hold values from -0.1875 to 0.1875
- w_down: bfloat16 [64, 1408, 2048], P('wide', None, 'narrow'), may hold values from -0.15625 to 0.15625
Outputs:
- combined: bfloat16 [4096, 2048], P('wide', 'narrow')
The draws below stay inside these ranges and needn't reach their ends.
Inputs may be any that keep to these rules, and one draw needn't show every extreme that they name: `routes`: each row names 6 different experts. Within each aligned block of 64 rows no expert is named by more than 11 rows, and in some block an expert is named by exactly 11 rows.
All inputs are finite; a program needn't handle non-finite values.
Results may differ from the reference program's by a relative error of at most 0.029.
Values may be sent and summed in bfloat16 or wider, within the bound.
No kernel may reach another device: no remote copies, remote signals or barrier semaphores. Data moves between devices by JAX's collectives and lax.ppermute only.
A program may use at most 64 MiB of HBM per device.

```python
import math
import jax
import jax.numpy as jnp
import numpy as np
from jax import lax

D = 2048
FF = 1408
TOP = 6
TOK_DEV = 64
EXPERTS = 64
TOKENS = 4096
CAP = 11
N_WIDE = 64
N_NARROW = 8


def raised(result, rng, source, target, shards_of, factor):
    owner, partner = [(jnp.arange(result.shape[axis_at]) // (result.shape[axis_at] // shards_of)).reshape([-1 if axis == axis_at else 1 for axis in range(result.ndim)]) for axis_at in (source, target)]
    chosen = jax.random.permutation(rng, shards_of)[partner]
    strong = (owner == chosen) | (owner == (partner + shards_of // 2) % shards_of)
    return jnp.where(strong, factor * result, result)


def block_scale(key, dims, split, smallest, top_value):
    loudness = 1.0
    for dim, blocks in split:
        steps = jax.random.uniform(jax.random.fold_in(jax.random.fold_in(key, 6), dim), (blocks,), jnp.float32, smallest / len(split), top_value / len(split))
        loudness = loudness * jnp.repeat(jnp.exp(steps), dims[dim] // blocks).reshape((-1,) + (1,) * (len(dims) - 1 - dim))
    return loudness


def routed_block(own_key, own, number, rows, count, top, limit, slope):
    ranking = jax.random.permutation(own_key, count)
    packed, ordinary = shares(count, rows * top, limit, slope, True), shares(count, rows * top, limit, slope, False)
    places = jnp.arange(count)

    def named(lengths, turn):
        used = int((lengths > 0).sum())
        fixed = max(1, used // 4)
        passed = fixed + (places - fixed + turn * (used - fixed)) % max(1, count - fixed)
        return jnp.zeros((count,), jnp.int32).at[ranking[jnp.where(places < fixed, places, passed)]].set(jnp.asarray(lengths, jnp.int32))

    lengths = jnp.where(number % 4 == 0, named(packed, number // 4), named(ordinary, number - number // 4 - 1))
    mixed = jax.random.permutation(jax.random.fold_in(own, 3), count)
    source_of, taker = mixed[0:count // 2 * 2:2], mixed[1:count // 2 * 2:2]
    margin = jnp.minimum(lengths[source_of] - 1, limit - lengths[taker]) // 2
    margin = jnp.where((source_of == ranking[0]) | (taker == ranking[0]) | (lengths[taker] == 0), 0, jnp.maximum(margin, 0))
    passed = jax.random.randint(jax.random.fold_in(own, 4), (count // 2,), 0, 1 << 20) % (margin + 1)
    lengths = lengths.at[source_of].add(-passed).at[taker].add(passed)
    members = jnp.searchsorted(jnp.cumsum(lengths), jnp.arange(rows * top), side="right").astype(jnp.int32)
    grid = members.reshape(top, rows).T
    grid = grid[jax.random.permutation(jax.random.fold_in(own, 1), rows)]
    turn = jax.random.randint(jax.random.fold_in(own, 2), (rows, 1), 0, top)
    return jnp.take_along_axis(grid, (jnp.arange(top)[None, :] + turn) % top, axis=1)


def shares(number_of, total, reach, slope, full):
    loads = [(1 << 20) // math.isqrt(grade ** slope) + 1 for grade in range(1, number_of + 1)]
    largest = reach if full else min(reach, max(-(-total // number_of), total * loads[0] // sum(loads)))
    least = 1 if total - largest >= number_of - 1 else 0
    holding, surplus = [largest] + [least] * (number_of - 1), total - largest - least * (number_of - 1)
    while surplus > 0:
        free = [i for i in range(1, number_of) if holding[i] < largest] or [i for i in range(1, number_of) if holding[i] < reach]
        mass, remaining = sum([loads[i] for i in free]), surplus
        for i in free:
            addition = min(reach - holding[i], max(1, remaining * loads[i] // mass), surplus)
            holding[i] = holding[i] + addition
            surplus = surplus - addition
    return np.array(holding)


def normal_values(rng, dims, spread, bound, shards=(), held_as=jnp.bfloat16):
    array = jax.random.normal(rng, dims, jnp.float32) * spread
    if len(shards) > 0:
        array = block_scale(rng, dims, shards, -0.22, 0.18) * array
    return jnp.clip(array, min=-bound, max=bound).astype(held_as)


def bell_draw_with(stream_key, shape, deviation, reach, split, heavy, held_as=jnp.bfloat16):
    array = deviation * jax.random.normal(stream_key, shape, jnp.float32)
    if split:
        array = array * block_scale(stream_key, shape, split, -0.22, 0.18)
    return jnp.clip(raised(array, jax.random.fold_in(stream_key, 3), *heavy), -reach, reach).astype(held_as)


def setup_inputs(seed: int = 0) -> dict:
    keys = jax.random.split(jax.random.key(seed), 7)
    tokens = normal_values(keys[0], (TOKENS, D), 1.0, 6.0, ((0, 64),))
    routes_keys = jax.random.split(jax.random.fold_in(keys[1], 1), TOKENS // TOK_DEV)
    routes_turns = jax.random.permutation(jax.random.fold_in(keys[1], 3), TOKENS // TOK_DEV)
    routes = jax.vmap(lambda own, number: routed_block(jax.random.fold_in(keys[1], 2), own, number, TOK_DEV, EXPERTS, TOP, CAP, 2))(routes_keys, routes_turns).reshape((TOKENS, TOP))
    route_weight = jnp.clip(0.1 + 0.7 * jax.random.uniform(keys[2], (TOKENS, TOP), jnp.float32) ** block_scale(keys[2], (TOKENS, TOP), ((0, 64),), -0.2, 0.2), 0.1, 0.8)
    w_gate = bell_draw_with(keys[3], (EXPERTS, FF, D), D ** -0.5, 0.1875, ((0, 64), (2, 8)), (2, 1, 8, 2.0))
    w_up = bell_draw_with(keys[4], (EXPERTS, FF, D), D ** -0.5, 0.1875, ((0, 64), (2, 8)), (2, 1, 8, 2.0))
    w_down = normal_values(keys[5], (EXPERTS, FF, D), FF ** -0.5, 0.15625, ((0, 64), (2, 8)))
    return {"tokens": tokens, "routes": routes, "route_weight": route_weight, "w_gate": w_gate, "w_up": w_up, "w_down": w_down}


def slots_of(route_block):
    flat_routes = route_block.reshape(-1)
    onehot = (flat_routes[:, None] == jnp.arange(EXPERTS, dtype=jnp.int32)[None, :]).astype(jnp.int32)
    before = jnp.cumsum(onehot, 0) - onehot
    return jnp.sum(before * onehot, 1).reshape(route_block.shape).astype(jnp.int32)


def block_sums(rows_blocks, matrix, column_width):
    blocks = matrix.reshape(FF, N_NARROW, column_width).astype(jnp.float32)
    parts = jnp.einsum('snc,fnc->nsf', rows_blocks, blocks)
    parts = lax.optimization_barrier(parts.astype(jnp.bfloat16)).astype(jnp.float32)
    return jnp.sum(parts, 0)


def reference(tokens, routes, route_weight, w_gate, w_up, w_down):
    slot_count = N_WIDE * CAP
    column_width = D // N_NARROW
    route_blocks = routes.reshape(N_WIDE, TOK_DEV, TOP)
    slot = jax.vmap(slots_of)(route_blocks).reshape(TOKENS, TOP)
    source_block = (jnp.arange(TOKENS, dtype=jnp.int32) // TOK_DEV)[:, None]
    place = (routes * slot_count + source_block * CAP + slot).astype(jnp.int32)
    owner = jnp.broadcast_to(jnp.arange(TOKENS, dtype=jnp.int32)[:, None], (TOKENS, TOP))
    table = jnp.full((EXPERTS * slot_count,), TOKENS, dtype=jnp.int32)
    table = table.at[place.reshape(-1)].set(owner.reshape(-1)).reshape(EXPERTS, slot_count)
    padded = jnp.concatenate([tokens, jnp.zeros((1, D), tokens.dtype)], 0)

    def one_expert(inputs):
        row_index, gate_matrix, up_matrix, down_matrix = inputs
        rows = padded[row_index]
        rows_blocks = rows.reshape(slot_count, N_NARROW, column_width).astype(jnp.float32)
        gate = block_sums(rows_blocks, gate_matrix, column_width)
        up = block_sums(rows_blocks, up_matrix, column_width)
        hidden = (jax.nn.silu(gate) * up).astype(jnp.bfloat16)
        return jnp.dot(hidden, down_matrix, preferred_element_type=jnp.float32).astype(jnp.bfloat16)

    expert_out = lax.map(one_expert, (table, w_gate, w_up, w_down))
    flat_rows = expert_out.reshape(EXPERTS * slot_count, D)
    picked = flat_rows[place].astype(jnp.float32)
    combined = jnp.sum(route_weight[:, :, None] * picked, 1)
    return combined.astype(jnp.bfloat16)
```

```python
import functools

import jax
import jax.numpy as jnp
from jax import lax
from jax.experimental import pallas as pl
from jax.experimental.pallas import tpu as pltpu
from jax.sharding import Mesh
from jax.sharding import PartitionSpec as P

VMEM = pl.BlockSpec(memory_space=pltpu.VMEM)
SMEM = pl.BlockSpec(memory_space=pltpu.SMEM)
NT = (((1,), (1,)), ((), ()))
TN = (((0,), (0,)), ((), ()))


def call(body, outs, *operands, scalars=0):
    return pl.pallas_call(
        body,
        out_shape=outs,
        in_specs=[SMEM] * scalars + [VMEM] * (len(operands) - scalars),
        out_specs=jax.tree.map(lambda _: VMEM, outs),
        compiler_params=pltpu.CompilerParams(vmem_limit_bytes=16 << 20),
    )(*operands)


def dispatch_body(cap, chips, cols, place, routes_t, tokens, outgoing, target_t):
    top, rows = routes_t.shape
    slots = outgoing.shape[0]
    experts = slots // cap
    expert_ids = lax.broadcasted_iota(jnp.int32, (experts, rows), 0)
    chosen = [(routes_t[k : k + 1, :] == expert_ids).astype(jnp.float32) for k in range(top)]
    named = functools.reduce(jnp.add, chosen)
    earlier = (
        lax.broadcasted_iota(jnp.int32, (rows, rows), 0) < lax.broadcasted_iota(jnp.int32, (rows, rows), 1)
    ).astype(jnp.bfloat16)
    before = jnp.dot(named.astype(jnp.bfloat16), earlier, preferred_element_type=jnp.float32)
    slot_ids = lax.broadcasted_iota(jnp.int32, (slots, rows), 0)
    picker = jnp.zeros((slots, rows), jnp.float32)
    for k in range(top):
        slot = jnp.sum(chosen[k] * before, axis=0, keepdims=True).astype(jnp.int32)
        target = routes_t[k : k + 1, :] * cap + slot
        target_t[k : k + 1, :] = target
        picker += (slot_ids == target).astype(jnp.float32)
    picker = picker.astype(jnp.bfloat16)
    parts = []
    for shift in range(chips):
        block = lax.rem(place[0] - shift + chips, chips) * 2 + place[1]
        columns = tokens[:, pl.ds(pl.multiple_of(block * cols, cols), cols)]
        parts.append(jnp.dot(picker, columns, preferred_element_type=jnp.float32).astype(jnp.bfloat16))
    outgoing[...] = jnp.concatenate(parts, 1).reshape(outgoing.shape)


def gate_up_body(cols, place, rows, *refs):
    weights, (theirs, mine) = refs[:-2], refs[-2:]
    half = mine.shape[0]
    flat = rows[...].reshape(rows.shape[0], rows.shape[1] * rows.shape[2])
    total = functools.reduce(
        jnp.add,
        [
            lax.dot_general(
                flat[:, s * cols : (s + 1) * cols], w[...], NT, preferred_element_type=jnp.float32
            )
            for s, w in enumerate(weights)
        ],
    )
    first = place[1] == 0
    theirs[...] = jnp.where(first, total[half:], total[:half]).astype(jnp.bfloat16)
    mine[...] = jnp.where(first, total[:half], total[half:])


def hidden_body(mine, theirs, hidden):
    units = hidden.shape[1]
    total = mine[...] + theirs[...].astype(jnp.float32)
    gate, up = total[:, :units], total[:, units:]
    hidden[...] = (gate / (1 + jnp.exp(-gate)) * up).astype(jnp.bfloat16)


def down_body(place, own, other, w_down, out):
    chips, half, units = own.shape
    for source, which in ((own, place[1]), (other, 1 - place[1])):
        total = functools.reduce(
            jnp.add,
            [
                jnp.dot(
                    source[z], w_down[z * units : (z + 1) * units, :], preferred_element_type=jnp.float32
                )
                for z in range(chips)
            ],
        )
        out[pl.ds(which * half, half)] = total.astype(jnp.bfloat16).reshape(half, *out.shape[1:])


def combine_body(target_t, weight_t, returned, out):
    top, rows = target_t.shape
    slots = returned.shape[0]
    slot_ids = lax.broadcasted_iota(jnp.int32, (slots, rows), 0)
    spread = jnp.zeros((slots, rows), jnp.float32)
    for k in range(top):
        spread += jnp.where(slot_ids == target_t[k : k + 1, :], weight_t[k : k + 1, :], 0.0)
    high = spread.astype(jnp.bfloat16)
    low = (spread - high.astype(jnp.float32)).astype(jnp.bfloat16)
    flat = returned[...].reshape(slots, out.shape[1])
    total = lax.dot_general(high, flat, TN, preferred_element_type=jnp.float32)
    total += lax.dot_general(low, flat, TN, preferred_element_type=jnp.float32)
    out[...] = total.astype(jnp.bfloat16)


def on_device(wide, chips, tokens, routes, route_weight, w_gate, w_up, w_down):
    tok_count, top = routes.shape
    _, units, cols = w_gate.shape
    experts = functools.reduce(lambda a, b: a * b, [lax.axis_size(a) for a in wide])
    cap = max(2, (11 * tok_count + experts - 1) // experts)
    slots = experts * cap
    share = units // chips
    half = slots // 2
    bf16 = jnp.bfloat16
    chip, core = lax.axis_index("chip"), lax.axis_index("core")
    place = jnp.stack([chip, core]).astype(jnp.int32)

    def share_of(index):
        start = index * share
        return jnp.concatenate(
            [lax.dynamic_slice_in_dim(w[0], start, share, 0) for w in (w_gate, w_up)], 0
        )

    weights = [share_of(chip)]
    for shift in range(1, chips):
        piece = share_of(lax.rem(chip + shift, chips))
        weights.append(lax.ppermute(piece, "chip", [(i, (i + shift) % chips) for i in range(chips)]))

    outgoing, target_t = call(
        functools.partial(dispatch_body, cap, chips, cols),
        (
            jax.ShapeDtypeStruct((slots, chips * cols // 128, 128), bf16),
            jax.ShapeDtypeStruct((top, tok_count), jnp.int32),
        ),
        place,
        routes.T,
        tokens,
        scalars=1,
    )
    received = lax.all_to_all(outgoing, wide, split_axis=0, concat_axis=0, tiled=True)
    theirs, mine = call(
        functools.partial(gate_up_body, cols),
        (
            jax.ShapeDtypeStruct((half, 2 * share), bf16),
            jax.ShapeDtypeStruct((half, 2 * share), jnp.float32),
        ),
        place,
        received,
        *weights,
        scalars=1,
    )
    theirs = lax.ppermute(theirs, "core", [(0, 1), (1, 0)])
    hidden = call(hidden_body, jax.ShapeDtypeStruct((half, share), bf16), mine, theirs)
    own = lax.all_gather(hidden, "chip", axis=0)
    other = lax.ppermute(own, "core", [(0, 1), (1, 0)])
    produced = call(
        down_body,
        jax.ShapeDtypeStruct((slots, cols // 128, 128), bf16),
        place,
        own,
        other,
        w_down[0],
        scalars=1,
    )
    returned = lax.all_to_all(produced, wide, split_axis=0, concat_axis=0, tiled=True)
    return call(
        combine_body,
        jax.ShapeDtypeStruct((tok_count, cols), bf16),
        target_t,
        route_weight.T,
        returned,
    )


def solution(mesh):
    chips = mesh.shape["narrow"] // 2
    fine = Mesh(mesh.devices.reshape(mesh.shape["wide"], chips, 2), ("wide", "chip", "core"))
    narrow = ("chip", "core")
    return jax.shard_map(
        functools.partial(on_device, ("wide",), chips),
        mesh=fine,
        in_specs=(
            P("wide", None),
            P("wide", None),
            P("wide", None),
            P("wide", None, narrow),
            P("wide", None, narrow),
            P("wide", None, narrow),
        ),
        out_specs=P("wide", narrow),
        check_vma=False,
    )
```

```python
import functools

import jax
import jax.numpy as jnp
from jax import lax
from jax.experimental import pallas as pl
from jax.experimental.pallas import tpu as pltpu
from jax.sharding import Mesh
from jax.sharding import PartitionSpec as P

VMEM = pl.BlockSpec(memory_space=pltpu.VMEM)
SMEM = pl.BlockSpec(memory_space=pltpu.SMEM)
NT = (((1,), (1,)), ((), ()))
TN = (((0,), (0,)), ((), ()))


def call(body, outs, *operands, scalars=0, flops=None):
    cost = None if flops is None else pl.CostEstimate(flops=flops, transcendentals=0, bytes_accessed=0)
    return pl.pallas_call(
        body,
        out_shape=outs,
        in_specs=[SMEM] * scalars + [VMEM] * (len(operands) - scalars),
        out_specs=jax.tree.map(lambda _: VMEM, outs),
        compiler_params=pltpu.CompilerParams(vmem_limit_bytes=16 << 20),
        cost_estimate=cost,
    )(*operands)


def dispatch_body(cap, chips, cols, place, routes_t, tokens, outgoing, target_t):
    top, rows = routes_t.shape
    slots = outgoing.shape[0]
    experts = slots // cap
    expert_ids = lax.broadcasted_iota(jnp.int32, (experts, rows), 0)
    chosen = [(routes_t[k : k + 1, :] == expert_ids).astype(jnp.float32) for k in range(top)]
    named = functools.reduce(jnp.add, chosen)
    earlier = (
        lax.broadcasted_iota(jnp.int32, (rows, rows), 0) < lax.broadcasted_iota(jnp.int32, (rows, rows), 1)
    ).astype(jnp.bfloat16)
    before = jnp.dot(named.astype(jnp.bfloat16), earlier, preferred_element_type=jnp.float32)
    slot_ids = lax.broadcasted_iota(jnp.int32, (slots, rows), 0)
    picker = jnp.zeros((slots, rows), jnp.float32)
    for k in range(top):
        slot = jnp.sum(chosen[k] * before, axis=0, keepdims=True).astype(jnp.int32)
        target = routes_t[k : k + 1, :] * cap + slot
        target_t[k : k + 1, :] = target
        picker += (slot_ids == target).astype(jnp.float32)
    picker = picker.astype(jnp.bfloat16)
    parts = []
    for shift in range(chips):
        block = lax.rem(place[0] - shift + chips, chips) * 2 + place[1]
        columns = tokens[:, pl.ds(pl.multiple_of(block * cols, cols), cols)]
        parts.append(jnp.dot(picker, columns, preferred_element_type=jnp.float32).astype(jnp.bfloat16))
    outgoing[...] = jnp.concatenate(parts, 1).reshape(outgoing.shape)


def pack_body(place, w_gate, w_up, ahead, behind):
    share = ahead.shape[0] // 3
    chips = w_gate.shape[0] // share

    def units(w, shift):
        start = lax.rem(place[0] + shift, chips) * share
        return w[pl.ds(pl.multiple_of(start, 16), share), :]

    for out, near, far in ((ahead, 1, w_gate), (behind, chips - 1, w_up)):
        out[:share, :] = units(w_gate, near)
        out[share : 2 * share, :] = units(w_up, near)
        out[2 * share :, :] = units(far, 2)


def relay_body(before, after, gate, up):
    share = gate.shape[0]
    gate[...] = before[2 * share :, :]
    up[...] = after[2 * share :, :]


def gather_body(place, w_gate, w_up, before, after, far_gate, far_up, weights):
    share, cols = far_gate.shape
    here = pl.ds(pl.multiple_of(place[0] * share, 16), share)
    weights[:share, :cols] = w_gate[here, :]
    weights[share:, :cols] = w_up[here, :]
    weights[:, cols : 2 * cols] = before[: 2 * share, :]
    weights[:share, 2 * cols : 3 * cols] = far_gate[...]
    weights[share:, 2 * cols : 3 * cols] = far_up[...]
    weights[:, 3 * cols :] = after[: 2 * share, :]


def gate_up_body(place, rows, weights, theirs, mine):
    half = mine.shape[0]
    flat = rows[...].reshape(rows.shape[0], rows.shape[1] * rows.shape[2])
    total = lax.dot_general(flat, weights[...], NT, preferred_element_type=jnp.float32)
    first = place[1] == 0
    theirs[...] = jnp.where(first, total[half:], total[:half]).astype(jnp.bfloat16)
    mine[...] = jnp.where(first, total[:half], total[half:])


def hidden_body(mine, theirs, hidden):
    units = hidden.shape[1]
    total = mine[...] + theirs[...].astype(jnp.float32)
    gate, up = total[:, :units], total[:, units:]
    hidden[...] = (gate / (1 + jnp.exp(-gate)) * up).astype(jnp.bfloat16)


def down_body(place, w_down, *refs):
    out = refs[-1]
    half, units = refs[0].shape
    per = len(refs) // 2
    chips = w_down.shape[0] // units
    for pieces, which in ((refs[:per], place[1]), (refs[per:-1], 1 - place[1])):
        here, before, after, *far = [p[...] for p in pieces]
        total = jnp.zeros((half, w_down.shape[1]), jnp.float32)
        for shift, part in enumerate((here, before, jnp.concatenate(far, 0), after)):
            start = lax.rem(place[0] - shift + chips, chips) * units
            total += jnp.dot(
                part,
                w_down[pl.ds(pl.multiple_of(start, 16), units), :],
                preferred_element_type=jnp.float32,
            )
        out[pl.ds(which * half, half)] = total.astype(jnp.bfloat16).reshape(half, *out.shape[1:])


def combine_body(target_t, weight_t, returned, out):
    top, rows = target_t.shape
    slots = returned.shape[0]
    slot_ids = lax.broadcasted_iota(jnp.int32, (slots, rows), 0)
    spread = jnp.zeros((slots, rows), jnp.float32)
    for k in range(top):
        spread += jnp.where(slot_ids == target_t[k : k + 1, :], weight_t[k : k + 1, :], 0.0)
    high = spread.astype(jnp.bfloat16)
    low = (spread - high.astype(jnp.float32)).astype(jnp.bfloat16)
    flat = returned[...].reshape(slots, out.shape[1])
    total = lax.dot_general(high, flat, TN, preferred_element_type=jnp.float32)
    total += lax.dot_general(low, flat, TN, preferred_element_type=jnp.float32)
    out[...] = total.astype(jnp.bfloat16)


def on_device(wide, chips, tokens, routes, route_weight, w_gate, w_up, w_down):
    tok_count, top = routes.shape
    _, units, cols = w_gate.shape
    experts = functools.reduce(lambda a, b: a * b, [lax.axis_size(a) for a in wide])
    cap = max(2, (11 * tok_count + experts - 1) // experts)
    slots = experts * cap
    share = units // chips
    half = slots // 2
    bf16 = jnp.bfloat16
    chip, core = lax.axis_index("chip"), lax.axis_index("core")
    place = jnp.stack([chip, core]).astype(jnp.int32)

    forward = [(i, (i + 1) % chips) for i in range(chips)]
    backward = [(i, (i - 1) % chips) for i in range(chips)]
    swap = [(0, 1), (1, 0)]

    part = jax.ShapeDtypeStruct((share, cols), bf16)
    parts = jax.ShapeDtypeStruct((3 * share, cols), bf16)
    ahead, behind = call(pack_body, (parts, parts), place, w_gate[0], w_up[0], scalars=1)
    before = lax.ppermute(ahead, "chip", forward)
    after = lax.ppermute(behind, "chip", backward)
    far_gate, far_up = call(relay_body, (part, part), before, after, flops=30_000_000_000)
    far_gate = lax.ppermute(far_gate, "chip", forward)
    far_up = lax.ppermute(far_up, "chip", backward)
    weights = call(
        gather_body,
        jax.ShapeDtypeStruct((2 * share, chips * cols), bf16),
        place,
        w_gate[0],
        w_up[0],
        before,
        after,
        far_gate,
        far_up,
        scalars=1,
    )

    outgoing, target_t = call(
        functools.partial(dispatch_body, cap, chips, cols),
        (
            jax.ShapeDtypeStruct((slots, chips * cols // 128, 128), bf16),
            jax.ShapeDtypeStruct((top, tok_count), jnp.int32),
        ),
        place,
        routes.T,
        tokens,
        scalars=1,
    )
    received = lax.all_to_all(outgoing, wide, split_axis=0, concat_axis=0, tiled=True)
    theirs, mine = call(
        gate_up_body,
        (
            jax.ShapeDtypeStruct((half, 2 * share), bf16),
            jax.ShapeDtypeStruct((half, 2 * share), jnp.float32),
        ),
        place,
        received,
        weights,
        scalars=1,
    )
    theirs = lax.ppermute(theirs, "core", swap)
    hidden = call(hidden_body, jax.ShapeDtypeStruct((half, share), bf16), mine, theirs)
    one_back = lax.ppermute(hidden, "chip", forward)
    one_on = lax.ppermute(hidden, "chip", backward)
    quarter = half // 2
    far = (
        lax.ppermute(one_back[:quarter], "chip", forward),
        lax.ppermute(one_on[quarter:], "chip", backward),
    )
    own = (hidden, one_back, one_on, *far)
    produced = call(
        down_body,
        jax.ShapeDtypeStruct((slots, cols // 128, 128), bf16),
        place,
        w_down[0],
        *own,
        *[lax.ppermute(piece, "core", swap) for piece in own],
        scalars=1,
    )
    returned = lax.all_to_all(produced, wide, split_axis=0, concat_axis=0, tiled=True)
    return call(
        combine_body,
        jax.ShapeDtypeStruct((tok_count, cols), bf16),
        target_t,
        route_weight.T,
        returned,
    )


def solution(mesh):
    chips = mesh.shape["narrow"] // 2
    fine = Mesh(mesh.devices.reshape(mesh.shape["wide"], chips, 2), ("wide", "chip", "core"))
    narrow = ("chip", "core")
    return jax.shard_map(
        functools.partial(on_device, ("wide",), chips),
        mesh=fine,
        in_specs=(
            P("wide", None),
            P("wide", None),
            P("wide", None),
            P("wide", None, narrow),
            P("wide", None, narrow),
            P("wide", None, narrow),
        ),
        out_specs=P("wide", narrow),
        check_vma=False,
    )
```

```python
import functools

import jax
import jax.numpy as jnp
from jax import lax
from jax.experimental import pallas as pl
from jax.experimental.pallas import tpu as pltpu
from jax.sharding import Mesh
from jax.sharding import PartitionSpec as P

VMEM = pl.BlockSpec(memory_space=pltpu.VMEM)
ANY = pl.BlockSpec(memory_space=pl.ANY)
SMEM = pl.BlockSpec(memory_space=pltpu.SMEM)
SHARES = (0, 2, 3, 1)
PAIR = [(0, 1), (1, 0), (2, 3), (3, 2)]
OPPOSITE = [(0, 3), (3, 0), (1, 2), (2, 1)]
SWAP = [(0, 1), (1, 0)]
CORE, HALF, SHARE, BLOCK, PAIR_BLOCK = range(5)
NT = (((1,), (1,)), ((), ()))
TN = (((0,), (0,)), ((), ()))


def call(body, outs, *operands, scalars=0, space=VMEM, scratch=()):
    return pl.pallas_call(
        body,
        out_shape=outs,
        in_specs=[SMEM] * scalars + [space] * (len(operands) - scalars),
        out_specs=jax.tree.map(lambda _: VMEM, outs),
        scratch_shapes=scratch,
        compiler_params=pltpu.CompilerParams(vmem_limit_bytes=16 << 20),
    )(*operands)


def dispatch_body(cap, cols, place, routes_t, tokens, outgoing, target_t):
    top, rows = routes_t.shape
    slots = outgoing.shape[0]
    experts = slots // cap
    expert_ids = lax.broadcasted_iota(jnp.int32, (experts, rows), 0)
    chosen = [(routes_t[k : k + 1, :] == expert_ids).astype(jnp.float32) for k in range(top)]
    named = functools.reduce(jnp.add, chosen)
    earlier = (
        lax.broadcasted_iota(jnp.int32, (rows, rows), 0) < lax.broadcasted_iota(jnp.int32, (rows, rows), 1)
    ).astype(jnp.bfloat16)
    before = jnp.dot(named.astype(jnp.bfloat16), earlier, preferred_element_type=jnp.float32)
    slot_ids = lax.broadcasted_iota(jnp.int32, (slots, rows), 0)
    picker = jnp.zeros((slots, rows), jnp.float32)
    for k in range(top):
        slot = jnp.sum(chosen[k] * before, axis=0, keepdims=True).astype(jnp.int32)
        target = routes_t[k : k + 1, :] * cap + slot
        target_t[k : k + 1, :] = target
        picker += (slot_ids == target).astype(jnp.float32)
    picker = picker.astype(jnp.bfloat16)
    parts = []
    for block in (place[BLOCK], place[PAIR_BLOCK]):
        columns = tokens[:, pl.ds(pl.multiple_of(block * cols, cols), cols)]
        parts.append(jnp.dot(picker, columns, preferred_element_type=jnp.float32).astype(jnp.bfloat16))
    outgoing[...] = jnp.concatenate(parts, 1).reshape(outgoing.shape)


def pack_body(share, place, w_gate, w_up, out, sems):
    copies = []
    for n, w in ((0, w_gate), (1, w_up)):
        for part in range(2):
            start = pl.multiple_of((1 - place[HALF]) * 2 * share + part * share, 16)
            copies.append(
                pltpu.make_async_copy(
                    w.at[pl.ds(start, share), :],
                    out.at[pl.ds((2 * part + n) * share, share), :],
                    sems.at[2 * n + part],
                )
            )
    for copy in copies:
        copy.start()
    for copy in copies:
        copy.wait()


def gate_up_body(keep, place, rows, w_gate, w_up, pair, theirs, mine):
    half, both = mine.shape
    share = both // 2
    part = place[SHARE] if keep else 1 - place[SHARE]
    flat = rows[...].reshape(rows.shape[0], rows.shape[1] * rows.shape[2])
    here = pl.ds(pl.multiple_of((2 * place[HALF] + part) * share, 16), share)
    weights = jnp.concatenate(
        [
            jnp.concatenate([w_gate[here, :], w_up[here, :]], 0),
            pair[pl.ds(pl.multiple_of(part * both, 16), both), :],
        ],
        1,
    )
    total = lax.dot_general(flat, weights, NT, preferred_element_type=jnp.float32)
    first = place[CORE] == 0
    theirs[...] = jnp.where(first, total[half:], total[:half]).astype(jnp.bfloat16)
    mine[...] = jnp.where(first, total[:half], total[half:])


def add_body(mine, theirs, out):
    out[...] = (mine[...] + theirs[...].astype(jnp.float32)).astype(out.dtype)


def hidden_body(mine, theirs, far, hidden):
    units = hidden.shape[1]
    total = mine[...] + theirs[...].astype(jnp.float32) + far[...].astype(jnp.float32)
    gate, up = total[:, :units], total[:, units:]
    hidden[...] = (gate / (1 + jnp.exp(-gate)) * up).astype(jnp.bfloat16)


def down_body(place, own, other, w_down, out):
    half, units = own.shape[1:]
    for source, which in ((own, place[CORE]), (other, 1 - place[CORE])):
        total = functools.reduce(
            jnp.add,
            [
                jnp.dot(
                    source[z], w_down[n * units : (n + 1) * units, :], preferred_element_type=jnp.float32
                )
                for z, n in enumerate(SHARES)
            ],
        )
        out[pl.ds(which * half, half)] = total.astype(jnp.bfloat16).reshape(half, *out.shape[1:])


def combine_body(target_t, weight_t, returned, out):
    top, rows = target_t.shape
    slots = returned.shape[0]
    slot_ids = lax.broadcasted_iota(jnp.int32, (slots, rows), 0)
    spread = jnp.zeros((slots, rows), jnp.float32)
    for k in range(top):
        spread += jnp.where(slot_ids == target_t[k : k + 1, :], weight_t[k : k + 1, :], 0.0)
    high = spread.astype(jnp.bfloat16)
    low = (spread - high.astype(jnp.float32)).astype(jnp.bfloat16)
    flat = returned[...].reshape(slots, out.shape[1])
    total = lax.dot_general(high, flat, TN, preferred_element_type=jnp.float32)
    total += lax.dot_general(low, flat, TN, preferred_element_type=jnp.float32)
    out[...] = total.astype(jnp.bfloat16)


def on_device(wide, chips, tokens, routes, route_weight, w_gate, w_up, w_down):
    tok_count, top = routes.shape
    _, units, cols = w_gate.shape
    experts = functools.reduce(lambda a, b: a * b, [lax.axis_size(a) for a in wide])
    cap = max(2, (11 * tok_count + experts - 1) // experts)
    slots = experts * cap
    share = units // chips
    half = slots // 2
    bf16 = jnp.bfloat16
    chip, core = lax.axis_index("chip"), lax.axis_index("core")
    quarter = 2 * ((chip ^ (chip >> 1)) & 1) + (chip >> 1)
    place = jnp.stack(
        [core, quarter >> 1, quarter & 1, 2 * chip + core, 2 * (chip ^ 1) + core]
    ).astype(jnp.int32)

    packed = call(
        functools.partial(pack_body, share),
        jax.ShapeDtypeStruct((4 * share, cols), bf16),
        place,
        w_gate[0],
        w_up[0],
        scalars=1,
        space=ANY,
        scratch=[pltpu.SemaphoreType.DMA((4,))],
    )
    pair = lax.ppermute(packed, "chip", PAIR)

    outgoing, target_t = call(
        functools.partial(dispatch_body, cap, cols),
        (
            jax.ShapeDtypeStruct((slots, 2 * cols // 128, 128), bf16),
            jax.ShapeDtypeStruct((top, tok_count), jnp.int32),
        ),
        place,
        routes.T,
        tokens,
        scalars=1,
    )
    received = lax.all_to_all(outgoing, wide, split_axis=0, concat_axis=0, tiled=True)
    sums = {}
    for keep in (False, True):
        theirs, mine = call(
            functools.partial(gate_up_body, keep),
            (
                jax.ShapeDtypeStruct((half, 2 * share), bf16),
                jax.ShapeDtypeStruct((half, 2 * share), jnp.float32),
            ),
            place,
            received,
            w_gate[0],
            w_up[0],
            pair,
            scalars=1,
        )
        sums[keep] = (mine, lax.ppermute(theirs, "core", SWAP))
    sent = call(add_body, jax.ShapeDtypeStruct((half, 2 * share), bf16), *sums[False])
    far = lax.ppermute(sent, "chip", OPPOSITE)
    hidden = call(hidden_body, jax.ShapeDtypeStruct((half, share), bf16), *sums[True], far)
    own = lax.all_gather(hidden, "chip", axis=0)
    other = lax.ppermute(own, "core", SWAP)
    produced = call(
        down_body,
        jax.ShapeDtypeStruct((slots, cols // 128, 128), bf16),
        place,
        own,
        other,
        w_down[0],
        scalars=1,
    )
    returned = lax.all_to_all(produced, wide, split_axis=0, concat_axis=0, tiled=True)
    return call(
        combine_body,
        jax.ShapeDtypeStruct((tok_count, cols), bf16),
        target_t,
        route_weight.T,
        returned,
    )


def solution(mesh):
    chips = mesh.shape["narrow"] // 2
    fine = Mesh(mesh.devices.reshape(mesh.shape["wide"], chips, 2), ("wide", "chip", "core"))
    narrow = ("chip", "core")
    return jax.shard_map(
        functools.partial(on_device, ("wide",), chips),
        mesh=fine,
        in_specs=(
            P("wide", None),
            P("wide", None),
            P("wide", None),
            P("wide", None, narrow),
            P("wide", None, narrow),
            P("wide", None, narrow),
        ),
        out_specs=P("wide", narrow),
        check_vma=False,
    )
```

```python
import functools

import jax
import jax.numpy as jnp
from jax import lax
from jax.experimental import pallas as pl
from jax.experimental.pallas import tpu as pltpu
from jax.sharding import Mesh
from jax.sharding import PartitionSpec as P

VMEM = pl.BlockSpec(memory_space=pltpu.VMEM)
SMEM = pl.BlockSpec(memory_space=pltpu.SMEM)
CHIPS = 4
RELAY = 30_000_000_000
CORE, CHIP, SIDE = range(3)
NT = (((1,), (1,)), ((), ()))
TN = (((0,), (0,)), ((), ()))


def call(body, outs, *operands, scalars=0, flops=None):
    cost = None if flops is None else pl.CostEstimate(flops=flops, transcendentals=0, bytes_accessed=0)
    return pl.pallas_call(
        body,
        out_shape=outs,
        in_specs=[SMEM] * scalars + [VMEM] * (len(operands) - scalars),
        out_specs=jax.tree.map(lambda _: VMEM, outs),
        compiler_params=pltpu.CompilerParams(vmem_limit_bytes=16 << 20),
        cost_estimate=cost,
    )(*operands)


def block_body(place, routes_t, tokens, out):
    rows = tokens.shape[0]
    cols = out.shape[1] // CHIPS
    out[rows:, :] = jnp.zeros((out.shape[0] - rows, out.shape[1]), out.dtype)
    for shift in range(CHIPS):
        block = lax.rem(place[CHIP] - shift + CHIPS, CHIPS) * 2 + place[CORE]
        columns = tokens[:, pl.ds(pl.multiple_of(block * cols, cols), cols)]
        out[:rows, shift * cols : (shift + 1) * cols] = columns
    out[rows : rows + routes_t.shape[0], : routes_t.shape[1]] = routes_t[...].astype(out.dtype)


def dispatch_body(top, cap, experts, place, mine, neighbour, outgoing, target_t):
    rows = target_t.shape[1]
    side = outgoing.shape[0]
    slots = side * cap
    expert_ids = lax.broadcasted_iota(jnp.int32, (experts, rows), 0)
    slot_ids = lax.broadcasted_iota(jnp.int32, (slots, rows), 0)
    earlier = (
        lax.broadcasted_iota(jnp.int32, (rows, rows), 0) < lax.broadcasted_iota(jnp.int32, (rows, rows), 1)
    ).astype(jnp.bfloat16)
    for block, which in ((mine, place[SIDE]), (neighbour, 1 - place[SIDE])):
        routes_t = block[rows : rows + 16, :rows].astype(jnp.float32).astype(jnp.int32)
        chosen = [(routes_t[k : k + 1, :] == expert_ids).astype(jnp.float32) for k in range(top)]
        named = functools.reduce(jnp.add, chosen)
        before = jnp.dot(named.astype(jnp.bfloat16), earlier, preferred_element_type=jnp.float32)
        picker = jnp.zeros((slots, rows), jnp.float32)
        for k in range(top):
            slot = jnp.sum(chosen[k] * before, axis=0, keepdims=True).astype(jnp.int32)
            target = routes_t[k : k + 1, :] * cap + slot
            if block is mine:
                target_t[k : k + 1, :] = target
            picker += (slot_ids == target - place[SIDE] * slots).astype(jnp.float32)
        picked = jnp.dot(picker.astype(jnp.bfloat16), block[:rows, :], preferred_element_type=jnp.float32)
        outgoing[:, which] = picked.astype(jnp.bfloat16).reshape(side, cap, *outgoing.shape[3:])


def pack_body(place, w_gate, w_up, ahead, behind):
    share = ahead.shape[0] // 3
    chips = w_gate.shape[0] // share

    def units(w, shift):
        start = lax.rem(place[CHIP] + shift, chips) * share
        return w[pl.ds(pl.multiple_of(start, 16), share), :]

    for out, near, far in ((ahead, 1, w_gate), (behind, chips - 1, w_up)):
        out[:share, :] = units(w_gate, near)
        out[share : 2 * share, :] = units(w_up, near)
        out[2 * share :, :] = units(far, 2)


def relay_body(before, after, gate, up):
    share = gate.shape[0]
    gate[...] = before[2 * share :, :]
    up[...] = after[2 * share :, :]


def gather_body(place, w_gate, w_up, before, after, far_gate, far_up, weights):
    share, cols = far_gate.shape
    here = pl.ds(pl.multiple_of(place[CHIP] * share, 16), share)
    weights[:share, :cols] = w_gate[here, :]
    weights[share:, :cols] = w_up[here, :]
    weights[:, cols : 2 * cols] = before[: 2 * share, :]
    weights[:share, 2 * cols : 3 * cols] = far_gate[...]
    weights[share:, 2 * cols : 3 * cols] = far_up[...]
    weights[:, 3 * cols :] = after[: 2 * share, :]


def gate_up_body(place, rows, weights, theirs, mine):
    half = mine.shape[0]
    flat = rows[...].reshape(2 * half, weights.shape[1])
    total = lax.dot_general(flat, weights[...], NT, preferred_element_type=jnp.float32)
    first = place[CORE] == 0
    theirs[...] = jnp.where(first, total[half:], total[:half]).astype(jnp.bfloat16)
    mine[...] = jnp.where(first, total[:half], total[half:])


def hidden_body(mine, theirs, hidden):
    units = hidden.shape[1]
    total = mine[...] + theirs[...].astype(jnp.float32)
    gate, up = total[:, :units], total[:, units:]
    hidden[...] = (gate / (1 + jnp.exp(-gate)) * up).astype(jnp.bfloat16)


def down_body(place, own, other, w_down, out):
    chips, half, units = own.shape
    blocks, cap = out.shape[:2]
    for source, which in ((own, place[CORE]), (other, 1 - place[CORE])):
        total = functools.reduce(
            jnp.add,
            [
                jnp.dot(
                    source[z], w_down[z * units : (z + 1) * units, :], preferred_element_type=jnp.float32
                )
                for z in range(chips)
            ],
        )
        total = total.astype(jnp.bfloat16).reshape(blocks // 4, 2, cap, *out.shape[2:])
        for side in range(2):
            out[pl.ds(side * (blocks // 2) + which * (blocks // 4), blocks // 4)] = total[:, side]


def combine_body(target_t, weight_t, returned, out):
    top, rows = target_t.shape
    slots = returned.shape[0] * returned.shape[1]
    slot_ids = lax.broadcasted_iota(jnp.int32, (slots, rows), 0)
    spread = jnp.zeros((slots, rows), jnp.float32)
    for k in range(top):
        spread += jnp.where(slot_ids == target_t[k : k + 1, :], weight_t[k : k + 1, :], 0.0)
    high = spread.astype(jnp.bfloat16)
    low = (spread - high.astype(jnp.float32)).astype(jnp.bfloat16)
    flat = returned[...].reshape(slots, out.shape[1])
    total = lax.dot_general(high, flat, TN, preferred_element_type=jnp.float32)
    total += lax.dot_general(low, flat, TN, preferred_element_type=jnp.float32)
    out[...] = total.astype(jnp.bfloat16)


def on_device(tokens, routes, route_weight, w_gate, w_up, w_down):
    tok_count, top = routes.shape
    _, units, cols = w_gate.shape
    side = lax.axis_size("plane")
    experts = 2 * side
    cap = max(2, (11 * tok_count + experts - 1) // experts)
    slots = experts * cap
    share = units // CHIPS
    half = slots // 2
    bf16 = jnp.bfloat16
    forward = [(i, (i + 1) % CHIPS) for i in range(CHIPS)]
    backward = [(i, (i - 1) % CHIPS) for i in range(CHIPS)]
    swap = [(0, 1), (1, 0)]
    place = jnp.stack([lax.axis_index(a) for a in ("core", "chip", "side")]).astype(jnp.int32)

    mine = call(
        block_body,
        jax.ShapeDtypeStruct((tok_count + 16, CHIPS * cols), bf16),
        place,
        routes.T,
        tokens,
        scalars=1,
    )
    neighbour = lax.ppermute(mine, "side", swap)
    part = jax.ShapeDtypeStruct((share, cols), bf16)
    parts = jax.ShapeDtypeStruct((3 * share, cols), bf16)
    ahead, behind = call(pack_body, (parts, parts), place, w_gate[0], w_up[0], scalars=1)
    before = lax.ppermute(ahead, "chip", forward)
    after = lax.ppermute(behind, "chip", backward)
    far_gate, far_up = call(relay_body, (part, part), before, after, flops=RELAY)
    far_gate = lax.ppermute(far_gate, "chip", forward)
    far_up = lax.ppermute(far_up, "chip", backward)
    weights = call(
        gather_body,
        jax.ShapeDtypeStruct((2 * share, CHIPS * cols), bf16),
        place,
        w_gate[0],
        w_up[0],
        before,
        after,
        far_gate,
        far_up,
        scalars=1,
    )
    outgoing, target_t = call(
        functools.partial(dispatch_body, top, cap, experts),
        (
            jax.ShapeDtypeStruct((side, 2, cap, CHIPS * cols // 128, 128), bf16),
            jax.ShapeDtypeStruct((top, tok_count), jnp.int32),
        ),
        place,
        mine,
        neighbour,
        scalars=1,
    )
    received = lax.all_to_all(outgoing, "plane", split_axis=0, concat_axis=0, tiled=True)
    theirs, mine = call(
        gate_up_body,
        (
            jax.ShapeDtypeStruct((half, 2 * share), bf16),
            jax.ShapeDtypeStruct((half, 2 * share), jnp.float32),
        ),
        place,
        received,
        weights,
        scalars=1,
    )
    theirs = lax.ppermute(theirs, "core", swap)
    hidden = call(hidden_body, jax.ShapeDtypeStruct((half, share), bf16), mine, theirs)
    own = lax.all_gather(hidden, "chip", axis=0)
    other = lax.ppermute(own, "core", swap)
    produced = call(
        down_body,
        jax.ShapeDtypeStruct((experts, cap, cols // 128, 128), bf16),
        place,
        own,
        other,
        w_down[0],
        scalars=1,
    )
    returned = lax.all_to_all(produced, ("side", "plane"), split_axis=0, concat_axis=0, tiled=True)
    return call(
        combine_body,
        jax.ShapeDtypeStruct((tok_count, cols), bf16),
        target_t,
        route_weight.T,
        returned,
    )


def solution(mesh):
    fine = Mesh(
        mesh.devices.reshape(2, mesh.shape["wide"] // 2, CHIPS, 2), ("side", "plane", "chip", "core")
    )
    wide, narrow = ("side", "plane"), ("chip", "core")
    return jax.shard_map(
        on_device,
        mesh=fine,
        in_specs=(
            P(wide, None),
            P(wide, None),
            P(wide, None),
            P(wide, None, narrow),
            P(wide, None, narrow),
            P(wide, None, narrow),
        ),
        out_specs=P(wide, narrow),
        check_vma=False,
    )
```

```python
import functools

import jax
import jax.numpy as jnp
from jax import lax
from jax.experimental import pallas as pl
from jax.experimental.pallas import tpu as pltpu
from jax.sharding import Mesh
from jax.sharding import PartitionSpec as P

VMEM = pl.BlockSpec(memory_space=pltpu.VMEM)
HBM = pl.BlockSpec(memory_space=pltpu.HBM)
SMEM = pl.BlockSpec(memory_space=pltpu.SMEM)
NT = (((1,), (1,)), ((), ()))
TN = (((0,), (0,)), ((), ()))


GATHER = 40_000_000_000
CHIPS = 4
CORE, CHIP = range(2)


def call(body, outs, *operands, scalars=0, raw=0, scratch=(), flops=None, out_space=VMEM):
    operands = list(operands)
    for n in range(scalars, scalars + raw):
        operands[n] = pltpu.with_memory_space_constraint(operands[n], pltpu.HBM)
    cost = None if flops is None else pl.CostEstimate(flops=flops, transcendentals=0, bytes_accessed=0)
    return pl.pallas_call(
        body,
        out_shape=outs,
        in_specs=[SMEM] * scalars + [HBM] * raw + [VMEM] * (len(operands) - scalars - raw),
        out_specs=jax.tree.map(lambda _: out_space, outs),
        scratch_shapes=scratch,
        cost_estimate=cost,
        compiler_params=pltpu.CompilerParams(vmem_limit_bytes=16 << 20),
    )(*operands)


def copy_all(pairs, sems):
    copies = [pltpu.make_async_copy(src, dst, sems.at[n]) for n, (src, dst) in enumerate(pairs)]
    for copy in copies:
        copy.start()
    return copies


def dispatch_body(cap, place, routes_hbm, tokens_hbm, outgoing, target_t, routes_t, tokens, sems):
    top, rows = routes_t.shape
    slots = outgoing.shape[0]
    experts = slots // cap
    cols = tokens.shape[1] // CHIPS
    pairs = [(routes_hbm, routes_t)]
    for shift in range(CHIPS):
        block = lax.rem(place[CHIP] - shift + CHIPS, CHIPS) * 2 + place[CORE]
        columns = pl.ds(pl.multiple_of(block * cols, cols), cols)
        pairs.append((tokens_hbm.at[:, columns], tokens.at[:, shift * cols : (shift + 1) * cols]))
    copies = copy_all(pairs, sems)
    copies[0].wait()
    expert_ids = lax.broadcasted_iota(jnp.int32, (experts, rows), 0)
    chosen = [(routes_t[k : k + 1, :] == expert_ids).astype(jnp.float32) for k in range(top)]
    named = functools.reduce(jnp.add, chosen)
    earlier = (
        lax.broadcasted_iota(jnp.int32, (rows, rows), 0) < lax.broadcasted_iota(jnp.int32, (rows, rows), 1)
    ).astype(jnp.bfloat16)
    before = jnp.dot(named.astype(jnp.bfloat16), earlier, preferred_element_type=jnp.float32)
    slot_ids = lax.broadcasted_iota(jnp.int32, (slots, rows), 0)
    picker = jnp.zeros((slots, rows), jnp.float32)
    for k in range(top):
        slot = jnp.sum(chosen[k] * before, axis=0, keepdims=True).astype(jnp.int32)
        target = routes_t[k : k + 1, :] * cap + slot
        target_t[k : k + 1, :] = target
        picker += (slot_ids == target).astype(jnp.float32)
    for copy in copies[1:]:
        copy.wait()
    picked = jnp.dot(picker.astype(jnp.bfloat16), tokens[...], preferred_element_type=jnp.float32)
    outgoing[...] = picked.astype(jnp.bfloat16).reshape(outgoing.shape)


def units_of(place, shift, share):
    start = lax.rem(place[CHIP] + shift, CHIPS) * share
    return pl.ds(pl.multiple_of(start, 16), share)


def pack_body(place, w_gate, w_up, _, *refs):
    outs, sems = refs[:-1], refs[-1]
    share = outs[0].shape[0] // 2
    pairs = []
    for shift, out in enumerate(outs, 1):
        pairs.append((w_gate.at[units_of(place, shift, share), :], out.at[:share, :]))
        pairs.append((w_up.at[units_of(place, shift, share), :], out.at[share:, :]))
    for copy in copy_all(pairs, sems):
        copy.wait()


def gather_body(place, w_gate, w_up, one, two, three, weights, sems):
    both, cols = one.shape
    share = both // 2
    copies = copy_all(
        [
            (w.at[units_of(place, 0, share), :], weights.at[n * share : (n + 1) * share, :cols])
            for n, w in enumerate((w_gate, w_up))
        ],
        sems,
    )
    for shift, piece in enumerate((one, two, three), 1):
        weights[:, shift * cols : (shift + 1) * cols] = piece[...]
    for copy in copies:
        copy.wait()


def gate_up_body(mine, place, rows, weights, out):
    half = out.shape[0]
    for core in range(2):
        start = (core if mine else 1 - core) * half

        @pl.when(place[CORE] == core)
        def _():
            flat = rows[start : start + half].reshape(half, weights.shape[1])
            total = lax.dot_general(flat, weights[...], NT, preferred_element_type=jnp.float32)
            out[...] = total.astype(out.dtype)


def hidden_body(mine, theirs, hidden):
    units = hidden.shape[1]
    total = mine[...] + theirs[...].astype(jnp.float32)
    gate, up = total[:, :units], total[:, units:]
    hidden[...] = (gate / (1 + jnp.exp(-gate)) * up).astype(jnp.bfloat16)


def down(hidden, w_down):
    units = hidden.shape[2]
    total = functools.reduce(
        jnp.add,
        [
            jnp.dot(
                hidden[z], w_down[z * units : (z + 1) * units, :], preferred_element_type=jnp.float32
            )
            for z in range(CHIPS)
        ],
    )
    return total.astype(jnp.bfloat16)


def down_own_body(own, w_down, out):
    out[...] = down(own, w_down)


def down_body(place, own, other, w_down, out):
    half = own.shape[0]
    for value, which in ((own[...], place[CORE]), (down(other, w_down), 1 - place[CORE])):
        out[pl.ds(pl.multiple_of(which * half, 16), half)] = value.reshape(half, *out.shape[1:])


def combine_body(target_t, weight_t, returned, out):
    top, rows = target_t.shape
    slots = returned.shape[0]
    slot_ids = lax.broadcasted_iota(jnp.int32, (slots, rows), 0)
    spread = jnp.zeros((slots, rows), jnp.float32)
    for k in range(top):
        spread += jnp.where(slot_ids == target_t[k : k + 1, :], weight_t[k : k + 1, :], 0.0)
    high = spread.astype(jnp.bfloat16)
    low = (spread - high.astype(jnp.float32)).astype(jnp.bfloat16)
    flat = returned[...].reshape(slots, out.shape[1])
    total = lax.dot_general(high, flat, TN, preferred_element_type=jnp.float32)
    total += lax.dot_general(low, flat, TN, preferred_element_type=jnp.float32)
    out[...] = total.astype(jnp.bfloat16)


def on_device(tokens, routes, route_weight, w_gate, w_up, w_down):
    tok_count, top = routes.shape
    _, units, cols = w_gate.shape
    experts = lax.axis_size("wide")
    cap = max(2, (11 * tok_count + experts - 1) // experts)
    slots = experts * cap
    share = units // CHIPS
    half = slots // 2
    bf16 = jnp.bfloat16
    dma = pltpu.SemaphoreType.DMA
    swap = [(0, 1), (1, 0)]
    place = jnp.stack([lax.axis_index(a) for a in ("core", "chip")]).astype(jnp.int32)

    outgoing, target_t = call(
        functools.partial(dispatch_body, cap),
        (
            jax.ShapeDtypeStruct((slots, CHIPS * cols // 128, 128), bf16),
            jax.ShapeDtypeStruct((top, tok_count), jnp.int32),
        ),
        place,
        routes.T,
        tokens,
        scalars=1,
        raw=2,
        scratch=[
            pltpu.VMEM((top, tok_count), jnp.int32),
            pltpu.VMEM((tok_count, CHIPS * cols), bf16),
            dma((1 + CHIPS,)),
        ],
    )
    received = lax.all_to_all(outgoing, "wide", split_axis=0, concat_axis=0, tiled=True)

    part = jax.ShapeDtypeStruct((2 * share, cols), bf16)
    pieces = call(
        pack_body,
        (part,) * (CHIPS - 1),
        place,
        w_gate[0],
        w_up[0],
        target_t,
        scalars=1,
        raw=2,
        scratch=[dma((2 * (CHIPS - 1),))],
        out_space=HBM,
    )
    pieces = [
        lax.ppermute(piece, "chip", [(i, (i + shift) % CHIPS) for i in range(CHIPS)])
        for shift, piece in enumerate(pieces, 1)
    ]
    weights = call(
        gather_body,
        jax.ShapeDtypeStruct((2 * share, CHIPS * cols), bf16),
        place,
        w_gate[0],
        w_up[0],
        *pieces,
        scalars=1,
        raw=2,
        scratch=[dma((2,))],
        flops=GATHER,
    )
    theirs = call(
        functools.partial(gate_up_body, False),
        jax.ShapeDtypeStruct((half, 2 * share), bf16),
        place,
        received,
        weights,
        scalars=1,
    )
    theirs = lax.ppermute(theirs, "core", swap)
    mine = call(
        functools.partial(gate_up_body, True),
        jax.ShapeDtypeStruct((half, 2 * share), jnp.float32),
        place,
        received,
        weights,
        scalars=1,
    )
    hidden = call(hidden_body, jax.ShapeDtypeStruct((half, share), bf16), mine, theirs)
    own = lax.all_gather(hidden, "chip", axis=0)
    other = lax.ppermute(own, "core", swap)
    produced = call(
        down_body,
        jax.ShapeDtypeStruct((slots, cols // 128, 128), bf16),
        place,
        call(down_own_body, jax.ShapeDtypeStruct((half, cols), bf16), own, w_down[0]),
        other,
        w_down[0],
        scalars=1,
    )
    returned = lax.all_to_all(produced, "wide", split_axis=0, concat_axis=0, tiled=True)
    return call(
        combine_body,
        jax.ShapeDtypeStruct((tok_count, cols), bf16),
        target_t,
        route_weight.T,
        returned,
    )


def solution(mesh):
    fine = Mesh(mesh.devices.reshape(mesh.shape["wide"], CHIPS, 2), ("wide", "chip", "core"))
    narrow = ("chip", "core")
    return jax.shard_map(
        on_device,
        mesh=fine,
        in_specs=(
            P("wide", None),
            P("wide", None),
            P("wide", None),
            P("wide", None, narrow),
            P("wide", None, narrow),
            P("wide", None, narrow),
        ),
        out_specs=P("wide", narrow),
        check_vma=False,
    )
```

```python
import functools

import jax
import jax.numpy as jnp
from jax import lax
from jax.experimental import pallas as pl
from jax.experimental.pallas import tpu as pltpu
from jax.sharding import Mesh
from jax.sharding import PartitionSpec as P

VMEM = pl.BlockSpec(memory_space=pltpu.VMEM)
HBM = pl.BlockSpec(memory_space=pltpu.HBM)
SMEM = pl.BlockSpec(memory_space=pltpu.SMEM)
NT = (((1,), (1,)), ((), ()))
TN = (((0,), (0,)), ((), ()))


PICK = 10_000_000_000
GATHER = 40_000_000_000
CHIPS = 4
CORE, CHIP, SIDE = range(3)


def call(body, outs, *operands, scalars=0, raw=0, scratch=(), flops=None, out_space=VMEM):
    operands = list(operands)
    for n in range(scalars, scalars + raw):
        operands[n] = pltpu.with_memory_space_constraint(operands[n], pltpu.HBM)
    cost = None if flops is None else pl.CostEstimate(flops=flops, transcendentals=0, bytes_accessed=0)
    return pl.pallas_call(
        body,
        out_shape=outs,
        in_specs=[SMEM] * scalars + [HBM] * raw + [VMEM] * (len(operands) - scalars - raw),
        out_specs=jax.tree.map(lambda _: out_space, outs),
        scratch_shapes=scratch,
        cost_estimate=cost,
        compiler_params=pltpu.CompilerParams(vmem_limit_bytes=16 << 20),
    )(*operands)


def copy_all(pairs, sems):
    copies = [pltpu.make_async_copy(src, dst, sems.at[n]) for n, (src, dst) in enumerate(pairs)]
    for copy in copies:
        copy.start()
    return copies


def units_of(place, shift, share):
    start = lax.rem(place[CHIP] + shift, CHIPS) * share
    return pl.ds(pl.multiple_of(start, 16), share)


def first_body(place, routes_hbm, tokens_hbm, w_gate, w_up, mine, one, two, three, routes_t, sems):
    top, rows = routes_t.shape
    cols = mine.shape[1] // CHIPS
    share = one.shape[0] // 2
    pairs = [(routes_hbm, routes_t)]
    for shift in range(CHIPS):
        block = lax.rem(place[CHIP] - shift + CHIPS, CHIPS) * 2 + place[CORE]
        columns = pl.ds(pl.multiple_of(block * cols, cols), cols)
        pairs.append((tokens_hbm.at[:, columns], mine.at[:rows, shift * cols : (shift + 1) * cols]))
    for shift, out in enumerate((one, two, three), 1):
        pairs.append((w_gate.at[units_of(place, shift, share), :], out.at[:share, :]))
        pairs.append((w_up.at[units_of(place, shift, share), :], out.at[share:, :]))
    copies = copy_all(pairs, sems)
    mine[rows:, :] = jnp.zeros((mine.shape[0] - rows, mine.shape[1]), mine.dtype)
    copies[0].wait()
    mine[rows : rows + top, :rows] = routes_t[...].astype(mine.dtype)
    for copy in copies[1:]:
        copy.wait()


def picked(top, cap, experts, side, place, block, target_t=None):
    rows = block.shape[0] - 16
    slots = side * cap
    routes_t = block[rows:, :rows].astype(jnp.float32).astype(jnp.int32)
    expert_ids = lax.broadcasted_iota(jnp.int32, (experts, rows), 0)
    chosen = [(routes_t[k : k + 1, :] == expert_ids).astype(jnp.float32) for k in range(top)]
    named = functools.reduce(jnp.add, chosen)
    earlier = (
        lax.broadcasted_iota(jnp.int32, (rows, rows), 0) < lax.broadcasted_iota(jnp.int32, (rows, rows), 1)
    ).astype(jnp.bfloat16)
    before = jnp.dot(named.astype(jnp.bfloat16), earlier, preferred_element_type=jnp.float32)
    slot_ids = lax.broadcasted_iota(jnp.int32, (slots, rows), 0)
    picker = jnp.zeros((slots, rows), jnp.float32)
    for k in range(top):
        slot = jnp.sum(chosen[k] * before, axis=0, keepdims=True).astype(jnp.int32)
        target = routes_t[k : k + 1, :] * cap + slot
        if target_t is not None:
            target_t[k : k + 1, :] = target
        picker += (slot_ids == target - place[SIDE] * slots).astype(jnp.float32)
    rows_out = jnp.dot(picker.astype(jnp.bfloat16), block[:rows, :], preferred_element_type=jnp.float32)
    return rows_out.astype(jnp.bfloat16).reshape(side, cap, block.shape[1] // 128, 128)


def own_body(sizes, place, mine, out, target_t):
    out[...] = picked(*sizes, place, mine, target_t)


def dispatch_body(sizes, place, own, neighbour, outgoing):
    outgoing[:, 1 - place[SIDE]] = picked(*sizes, place, neighbour)
    outgoing[:, place[SIDE]] = own[...]


def gather_body(place, w_gate, w_up, one, two, three, weights, sems):
    both, cols = one.shape
    share = both // 2
    copies = copy_all(
        [
            (w.at[units_of(place, 0, share), :], weights.at[n * share : (n + 1) * share, :cols])
            for n, w in enumerate((w_gate, w_up))
        ],
        sems,
    )
    for shift, piece in enumerate((one, two, three), 1):
        weights[:, shift * cols : (shift + 1) * cols] = piece[...]
    for copy in copies:
        copy.wait()


def gate_up_body(mine, place, rows, weights, out):
    half = out.shape[0]
    for core in range(2):
        start = (core if mine else 1 - core) * (rows.shape[0] // 2)

        @pl.when(place[CORE] == core)
        def _():
            flat = rows[start : start + rows.shape[0] // 2].reshape(half, weights.shape[1])
            total = lax.dot_general(flat, weights[...], NT, preferred_element_type=jnp.float32)
            out[...] = total.astype(out.dtype)


def hidden_body(mine, theirs, hidden):
    units = hidden.shape[1]
    total = mine[...] + theirs[...].astype(jnp.float32)
    gate, up = total[:, :units], total[:, units:]
    hidden[...] = (gate / (1 + jnp.exp(-gate)) * up).astype(jnp.bfloat16)


def down(hidden, w_down):
    units = hidden.shape[2]
    total = functools.reduce(
        jnp.add,
        [
            jnp.dot(
                hidden[z], w_down[z * units : (z + 1) * units, :], preferred_element_type=jnp.float32
            )
            for z in range(CHIPS)
        ],
    )
    return total.astype(jnp.bfloat16)


def down_own_body(own, w_down, out):
    out[...] = down(own, w_down)


def down_body(place, own, other, w_down, out):
    blocks, cap = out.shape[:2]
    part = blocks // 4
    for value, which in ((own[...], place[CORE]), (down(other, w_down), 1 - place[CORE])):
        value = value.reshape(part, 2, cap, *out.shape[2:])
        for side in range(2):
            out[pl.ds(side * (blocks // 2) + which * part, part)] = value[:, side]


def combine_body(target_t, weight_t, returned, out):
    top, rows = target_t.shape
    slots = returned.shape[0] * returned.shape[1]
    slot_ids = lax.broadcasted_iota(jnp.int32, (slots, rows), 0)
    spread = jnp.zeros((slots, rows), jnp.float32)
    for k in range(top):
        spread += jnp.where(slot_ids == target_t[k : k + 1, :], weight_t[k : k + 1, :], 0.0)
    high = spread.astype(jnp.bfloat16)
    low = (spread - high.astype(jnp.float32)).astype(jnp.bfloat16)
    flat = returned[...].reshape(slots, out.shape[1])
    total = lax.dot_general(high, flat, TN, preferred_element_type=jnp.float32)
    total += lax.dot_general(low, flat, TN, preferred_element_type=jnp.float32)
    out[...] = total.astype(jnp.bfloat16)


def on_device(tokens, routes, route_weight, w_gate, w_up, w_down):
    tok_count, top = routes.shape
    _, units, cols = w_gate.shape
    side = lax.axis_size("plane")
    experts = 2 * side
    cap = max(2, (11 * tok_count + experts - 1) // experts)
    slots = experts * cap
    share = units // CHIPS
    half = slots // 2
    bf16 = jnp.bfloat16
    dma = pltpu.SemaphoreType.DMA
    swap = [(0, 1), (1, 0)]
    place = jnp.stack([lax.axis_index(a) for a in ("core", "chip", "side")]).astype(jnp.int32)

    part = jax.ShapeDtypeStruct((2 * share, cols), bf16)
    mine, *pieces = call(
        first_body,
        (jax.ShapeDtypeStruct((tok_count + 16, CHIPS * cols), bf16),) + (part,) * (CHIPS - 1),
        place,
        routes.T,
        tokens,
        w_gate[0],
        w_up[0],
        scalars=1,
        raw=4,
        scratch=[pltpu.VMEM((top, tok_count), jnp.int32), dma((1 + CHIPS + 2 * (CHIPS - 1),))],
    )
    neighbour = lax.ppermute(mine, "side", swap)
    sizes = (top, cap, experts, side)
    chunk = (cap, CHIPS * cols // 128, 128)
    picked_own, target_t = call(
        functools.partial(own_body, sizes),
        (
            jax.ShapeDtypeStruct((side, *chunk), bf16),
            jax.ShapeDtypeStruct((top, tok_count), jnp.int32),
        ),
        place,
        mine,
        scalars=1,
    )
    outgoing = call(
        functools.partial(dispatch_body, sizes),
        jax.ShapeDtypeStruct((side, 2, *chunk), bf16),
        place,
        picked_own,
        neighbour,
        scalars=1,
        flops=PICK,
    )
    received = lax.all_to_all(outgoing, "plane", split_axis=0, concat_axis=0, tiled=True)
    pieces = [
        lax.ppermute(piece, "chip", [(i, (i + shift) % CHIPS) for i in range(CHIPS)])
        for shift, piece in enumerate(pieces, 1)
    ]
    weights = call(
        gather_body,
        jax.ShapeDtypeStruct((2 * share, CHIPS * cols), bf16),
        place,
        w_gate[0],
        w_up[0],
        *pieces,
        scalars=1,
        raw=2,
        scratch=[dma((2,))],
        flops=GATHER,
    )
    theirs = call(
        functools.partial(gate_up_body, False),
        jax.ShapeDtypeStruct((half, 2 * share), bf16),
        place,
        received,
        weights,
        scalars=1,
    )
    theirs = lax.ppermute(theirs, "core", swap)
    mine = call(
        functools.partial(gate_up_body, True),
        jax.ShapeDtypeStruct((half, 2 * share), jnp.float32),
        place,
        received,
        weights,
        scalars=1,
    )
    hidden = call(hidden_body, jax.ShapeDtypeStruct((half, share), bf16), mine, theirs)
    own = lax.all_gather(hidden, "chip", axis=0)
    other = lax.ppermute(own, "core", swap)
    produced = call(
        down_body,
        jax.ShapeDtypeStruct((experts, cap, cols // 128, 128), bf16),
        place,
        call(down_own_body, jax.ShapeDtypeStruct((half, cols), bf16), own, w_down[0]),
        other,
        w_down[0],
        scalars=1,
    )
    returned = lax.all_to_all(produced, ("side", "plane"), split_axis=0, concat_axis=0, tiled=True)
    return call(
        combine_body,
        jax.ShapeDtypeStruct((tok_count, cols), bf16),
        target_t,
        route_weight.T,
        returned,
    )


def solution(mesh):
    fine = Mesh(
        mesh.devices.reshape(2, mesh.shape["wide"] // 2, CHIPS, 2), ("side", "plane", "chip", "core")
    )
    wide, narrow = ("side", "plane"), ("chip", "core")
    return jax.shard_map(
        on_device,
        mesh=fine,
        in_specs=(
            P(wide, None),
            P(wide, None),
            P(wide, None),
            P(wide, None, narrow),
            P(wide, None, narrow),
            P(wide, None, narrow),
        ),
        out_specs=P(wide, narrow),
        check_vma=False,
    )
```

```python
import functools

import jax
import jax.numpy as jnp
from jax import lax
from jax.experimental import pallas as pl
from jax.experimental.pallas import tpu as pltpu
from jax.sharding import Mesh
from jax.sharding import PartitionSpec as P

VMEM = pl.BlockSpec(memory_space=pltpu.VMEM)
HBM = pl.BlockSpec(memory_space=pltpu.HBM)
SMEM = pl.BlockSpec(memory_space=pltpu.SMEM)
NT = (((1,), (1,)), ((), ()))
TN = (((0,), (0,)), ((), ()))


GATHER = 20_000_000_000
CHIPS = 4
CORE, CHIP, SIDE = range(3)


def call(body, outs, *operands, scalars=0, raw=0, scratch=(), flops=None, out_space=VMEM):
    operands = list(operands)
    for n in range(scalars, scalars + raw):
        operands[n] = pltpu.with_memory_space_constraint(operands[n], pltpu.HBM)
    cost = None if flops is None else pl.CostEstimate(flops=flops, transcendentals=0, bytes_accessed=0)
    return pl.pallas_call(
        body,
        out_shape=outs,
        in_specs=[SMEM] * scalars + [HBM] * raw + [VMEM] * (len(operands) - scalars - raw),
        out_specs=jax.tree.map(lambda _: out_space, outs),
        scratch_shapes=scratch,
        cost_estimate=cost,
        compiler_params=pltpu.CompilerParams(vmem_limit_bytes=16 << 20),
    )(*operands)


def copy_all(pairs, sems):
    copies = [pltpu.make_async_copy(src, dst, sems.at[n]) for n, (src, dst) in enumerate(pairs)]
    for copy in copies:
        copy.start()
    return copies


def units_of(place, shift, share):
    start = lax.rem(place[CHIP] + shift, CHIPS) * share
    return pl.ds(pl.multiple_of(start, 16), share)


def first_body(place, routes_hbm, tokens_hbm, w_gate, w_up, mine, one, two, three, routes_t, sems):
    top, rows = routes_t.shape
    cols = mine.shape[1] // CHIPS
    share = one.shape[0] // 2
    pairs = [(routes_hbm, routes_t)]
    for shift in range(CHIPS):
        block = lax.rem(place[CHIP] - shift + CHIPS, CHIPS) * 2 + place[CORE]
        columns = pl.ds(pl.multiple_of(block * cols, cols), cols)
        pairs.append((tokens_hbm.at[:, columns], mine.at[:rows, shift * cols : (shift + 1) * cols]))
    for shift, out in enumerate((one, two, three), 1):
        pairs.append((w_gate.at[units_of(place, shift, share), :], out.at[:share, :]))
        pairs.append((w_up.at[units_of(place, shift, share), :], out.at[share:, :]))
    copies = copy_all(pairs, sems)
    mine[rows:, :] = jnp.zeros((mine.shape[0] - rows, mine.shape[1]), mine.dtype)
    copies[0].wait()
    mine[rows : rows + top, :rows] = routes_t[...].astype(mine.dtype)
    for copy in copies[1:]:
        copy.wait()


def picked(top, cap, experts, side, place, block, target_t=None):
    rows = block.shape[0] - 16
    slots = side * cap
    routes_t = block[rows:, :rows].astype(jnp.float32).astype(jnp.int32)
    expert_ids = lax.broadcasted_iota(jnp.int32, (experts, rows), 0)
    chosen = [(routes_t[k : k + 1, :] == expert_ids).astype(jnp.float32) for k in range(top)]
    named = functools.reduce(jnp.add, chosen)
    earlier = (
        lax.broadcasted_iota(jnp.int32, (rows, rows), 0) < lax.broadcasted_iota(jnp.int32, (rows, rows), 1)
    ).astype(jnp.bfloat16)
    before = jnp.dot(named.astype(jnp.bfloat16), earlier, preferred_element_type=jnp.float32)
    slot_ids = lax.broadcasted_iota(jnp.int32, (slots, rows), 0)
    picker = jnp.zeros((slots, rows), jnp.float32)
    for k in range(top):
        slot = jnp.sum(chosen[k] * before, axis=0, keepdims=True).astype(jnp.int32)
        target = routes_t[k : k + 1, :] * cap + slot
        if target_t is not None:
            target_t[k : k + 1, :] = target
        picker += (slot_ids == target - place[SIDE] * slots).astype(jnp.float32)
    rows_out = jnp.dot(picker.astype(jnp.bfloat16), block[:rows, :], preferred_element_type=jnp.float32)
    return rows_out.astype(jnp.bfloat16).reshape(side, cap, block.shape[1] // 128, 128)


def own_body(sizes, place, mine, out, target_t):
    out[...] = picked(*sizes, place, mine, target_t)


def dispatch_body(sizes, place, own, neighbour, outgoing):
    outgoing[:, 1 - place[SIDE]] = picked(*sizes, place, neighbour)
    outgoing[:, place[SIDE]] = own[...]


def gather_body(place, w_gate, w_up, one, two, three, weights, sems):
    both, cols = one.shape
    share = both // 2
    copies = copy_all(
        [
            (w.at[units_of(place, 0, share), :], weights.at[n * share : (n + 1) * share, :cols])
            for n, w in enumerate((w_gate, w_up))
        ],
        sems,
    )
    for shift, piece in enumerate((one, two, three), 1):
        weights[:, shift * cols : (shift + 1) * cols] = piece[...]
    for copy in copies:
        copy.wait()


def gate_up_body(mine, place, rows, weights, out):
    half = out.shape[0]
    for core in range(2):
        start = (core if mine else 1 - core) * (rows.shape[0] // 2)

        @pl.when(place[CORE] == core)
        def _():
            flat = rows[start : start + rows.shape[0] // 2].reshape(half, weights.shape[1])
            total = lax.dot_general(flat, weights[...], NT, preferred_element_type=jnp.float32)
            out[...] = total.astype(out.dtype)


def hidden_body(mine, theirs, hidden):
    units = hidden.shape[1]
    total = mine[...] + theirs[...].astype(jnp.float32)
    gate, up = total[:, :units], total[:, units:]
    hidden[...] = (gate / (1 + jnp.exp(-gate)) * up).astype(jnp.bfloat16)


def down(hidden, w_down):
    units = hidden.shape[2]
    total = functools.reduce(
        jnp.add,
        [
            jnp.dot(
                hidden[z], w_down[z * units : (z + 1) * units, :], preferred_element_type=jnp.float32
            )
            for z in range(CHIPS)
        ],
    )
    return total.astype(jnp.bfloat16)


def down_own_body(own, w_down, out):
    out[...] = down(own, w_down)


def down_body(place, own, other, w_down, out):
    blocks, cap = out.shape[:2]
    part = blocks // 4
    for value, which in ((own[...], place[CORE]), (down(other, w_down), 1 - place[CORE])):
        value = value.reshape(part, 2, cap, *out.shape[2:])
        for side in range(2):
            out[pl.ds(side * (blocks // 2) + which * part, part)] = value[:, side]


def combine_body(target_t, weight_t, returned, out):
    top, rows = target_t.shape
    slots = returned.shape[0] * returned.shape[1]
    slot_ids = lax.broadcasted_iota(jnp.int32, (slots, rows), 0)
    spread = jnp.zeros((slots, rows), jnp.float32)
    for k in range(top):
        spread += jnp.where(slot_ids == target_t[k : k + 1, :], weight_t[k : k + 1, :], 0.0)
    high = spread.astype(jnp.bfloat16)
    low = (spread - high.astype(jnp.float32)).astype(jnp.bfloat16)
    flat = returned[...].reshape(slots, out.shape[1])
    total = lax.dot_general(high, flat, TN, preferred_element_type=jnp.float32)
    total += lax.dot_general(low, flat, TN, preferred_element_type=jnp.float32)
    out[...] = total.astype(jnp.bfloat16)


def on_device(tokens, routes, route_weight, w_gate, w_up, w_down):
    tok_count, top = routes.shape
    _, units, cols = w_gate.shape
    side = lax.axis_size("plane")
    experts = 2 * side
    cap = max(2, (11 * tok_count + experts - 1) // experts)
    slots = experts * cap
    share = units // CHIPS
    half = slots // 2
    bf16 = jnp.bfloat16
    dma = pltpu.SemaphoreType.DMA
    swap = [(0, 1), (1, 0)]
    place = jnp.stack([lax.axis_index(a) for a in ("core", "chip", "side")]).astype(jnp.int32)

    part = jax.ShapeDtypeStruct((2 * share, cols), bf16)
    mine, *pieces = call(
        first_body,
        (jax.ShapeDtypeStruct((tok_count + 16, CHIPS * cols), bf16),) + (part,) * (CHIPS - 1),
        place,
        routes.T,
        tokens,
        w_gate[0],
        w_up[0],
        scalars=1,
        raw=4,
        scratch=[pltpu.VMEM((top, tok_count), jnp.int32), dma((1 + CHIPS + 2 * (CHIPS - 1),))],
    )
    neighbour = lax.ppermute(mine, "side", swap)
    sizes = (top, cap, experts, side)
    chunk = (cap, CHIPS * cols // 128, 128)
    picked_own, target_t = call(
        functools.partial(own_body, sizes),
        (
            jax.ShapeDtypeStruct((side, *chunk), bf16),
            jax.ShapeDtypeStruct((top, tok_count), jnp.int32),
        ),
        place,
        mine,
        scalars=1,
    )
    outgoing = call(
        functools.partial(dispatch_body, sizes),
        jax.ShapeDtypeStruct((side, 2, *chunk), bf16),
        place,
        picked_own,
        neighbour,
        scalars=1,
    )
    received = lax.all_to_all(outgoing, "plane", split_axis=0, concat_axis=0, tiled=True)
    pieces = [
        lax.ppermute(piece, "chip", [(i, (i + shift) % CHIPS) for i in range(CHIPS)])
        for shift, piece in enumerate(pieces, 1)
    ]
    weights = call(
        gather_body,
        jax.ShapeDtypeStruct((2 * share, CHIPS * cols), bf16),
        place,
        w_gate[0],
        w_up[0],
        *pieces,
        scalars=1,
        raw=2,
        scratch=[dma((2,))],
        flops=GATHER,
    )
    theirs = call(
        functools.partial(gate_up_body, False),
        jax.ShapeDtypeStruct((half, 2 * share), bf16),
        place,
        received,
        weights,
        scalars=1,
    )
    theirs = lax.ppermute(theirs, "core", swap)
    mine = call(
        functools.partial(gate_up_body, True),
        jax.ShapeDtypeStruct((half, 2 * share), jnp.float32),
        place,
        received,
        weights,
        scalars=1,
    )
    hidden = call(hidden_body, jax.ShapeDtypeStruct((half, share), bf16), mine, theirs)
    own = lax.all_gather(hidden, "chip", axis=0)
    other = lax.ppermute(own, "core", swap)
    produced = call(
        down_body,
        jax.ShapeDtypeStruct((experts, cap, cols // 128, 128), bf16),
        place,
        call(down_own_body, jax.ShapeDtypeStruct((half, cols), bf16), own, w_down[0]),
        other,
        w_down[0],
        scalars=1,
    )
    returned = lax.all_to_all(produced, ("side", "plane"), split_axis=0, concat_axis=0, tiled=True)
    return call(
        combine_body,
        jax.ShapeDtypeStruct((tok_count, cols), bf16),
        target_t,
        route_weight.T,
        returned,
    )


def solution(mesh):
    fine = Mesh(
        mesh.devices.reshape(2, mesh.shape["wide"] // 2, CHIPS, 2), ("side", "plane", "chip", "core")
    )
    wide, narrow = ("side", "plane"), ("chip", "core")
    return jax.shard_map(
        on_device,
        mesh=fine,
        in_specs=(
            P(wide, None),
            P(wide, None),
            P(wide, None),
            P(wide, None, narrow),
            P(wide, None, narrow),
            P(wide, None, narrow),
        ),
        out_specs=P(wide, narrow),
        check_vma=False,
    )
```

```python
import functools

import jax
import jax.numpy as jnp
from jax import lax
from jax.experimental import pallas as pl
from jax.experimental.pallas import tpu as pltpu
from jax.sharding import Mesh
from jax.sharding import PartitionSpec as P

VMEM = pl.BlockSpec(memory_space=pltpu.VMEM)
HBM = pl.BlockSpec(memory_space=pltpu.HBM)
SMEM = pl.BlockSpec(memory_space=pltpu.SMEM)
NT = (((1,), (1,)), ((), ()))
TN = (((0,), (0,)), ((), ()))


PACK = 30_000_000_000
PICK = 10_000_000_000
CHIPS = 4
CORE, CHIP, SIDE = range(3)


def call(body, outs, *operands, scalars=0, raw=0, scratch=(), flops=None, out_space=VMEM):
    operands = list(operands)
    for n in range(scalars, scalars + raw):
        operands[n] = pltpu.with_memory_space_constraint(operands[n], pltpu.HBM)
    cost = None if flops is None else pl.CostEstimate(flops=flops, transcendentals=0, bytes_accessed=0)
    return pl.pallas_call(
        body,
        out_shape=outs,
        in_specs=[SMEM] * scalars + [HBM] * raw + [VMEM] * (len(operands) - scalars - raw),
        out_specs=jax.tree.map(lambda _: out_space, outs),
        scratch_shapes=scratch,
        cost_estimate=cost,
        compiler_params=pltpu.CompilerParams(vmem_limit_bytes=16 << 20),
    )(*operands)


def copy_all(pairs, sems):
    copies = [pltpu.make_async_copy(src, dst, sems.at[n]) for n, (src, dst) in enumerate(pairs)]
    for copy in copies:
        copy.start()
    return copies


def units_of(place, shift, share):
    start = lax.rem(place[CHIP] + shift, CHIPS) * share
    return pl.ds(pl.multiple_of(start, 16), share)


def first_body(place, routes_hbm, tokens_hbm, w_gate, w_up, mine, two, routes_t, sems):
    top, rows = routes_t.shape
    cols = mine.shape[1] // CHIPS
    share = two.shape[0] // 2
    pairs = [(routes_hbm, routes_t)]
    for shift in range(CHIPS):
        block = lax.rem(place[CHIP] - shift + CHIPS, CHIPS) * 2 + place[CORE]
        columns = pl.ds(pl.multiple_of(block * cols, cols), cols)
        pairs.append((tokens_hbm.at[:, columns], mine.at[:rows, shift * cols : (shift + 1) * cols]))
    pairs.append((w_gate.at[units_of(place, 2, share), :], two.at[:share, :]))
    pairs.append((w_up.at[units_of(place, 2, share), :], two.at[share:, :]))
    copies = copy_all(pairs, sems)
    mine[rows:, :] = jnp.zeros((mine.shape[0] - rows, mine.shape[1]), mine.dtype)
    copies[0].wait()
    mine[rows : rows + top, :rows] = routes_t[...].astype(mine.dtype)
    for copy in copies[1:]:
        copy.wait()


def pack_body(place, w_gate, w_up, _, one, three, sems):
    share = one.shape[0] // 2
    pairs = []
    for shift, out in ((1, one), (3, three)):
        pairs.append((w_gate.at[units_of(place, shift, share), :], out.at[:share, :]))
        pairs.append((w_up.at[units_of(place, shift, share), :], out.at[share:, :]))
    for copy in copy_all(pairs, sems):
        copy.wait()


def picked(top, cap, experts, side, place, block, target_t=None):
    rows = block.shape[0] - 16
    slots = side * cap
    routes_t = block[rows:, :rows].astype(jnp.float32).astype(jnp.int32)
    expert_ids = lax.broadcasted_iota(jnp.int32, (experts, rows), 0)
    chosen = [(routes_t[k : k + 1, :] == expert_ids).astype(jnp.float32) for k in range(top)]
    named = functools.reduce(jnp.add, chosen)
    earlier = (
        lax.broadcasted_iota(jnp.int32, (rows, rows), 0) < lax.broadcasted_iota(jnp.int32, (rows, rows), 1)
    ).astype(jnp.bfloat16)
    before = jnp.dot(named.astype(jnp.bfloat16), earlier, preferred_element_type=jnp.float32)
    slot_ids = lax.broadcasted_iota(jnp.int32, (slots, rows), 0)
    picker = jnp.zeros((slots, rows), jnp.float32)
    for k in range(top):
        slot = jnp.sum(chosen[k] * before, axis=0, keepdims=True).astype(jnp.int32)
        target = routes_t[k : k + 1, :] * cap + slot
        if target_t is not None:
            target_t[k : k + 1, :] = target
        picker += (slot_ids == target - place[SIDE] * slots).astype(jnp.float32)
    rows_out = jnp.dot(picker.astype(jnp.bfloat16), block[:rows, :], preferred_element_type=jnp.float32)
    return rows_out.astype(jnp.bfloat16).reshape(side, cap, block.shape[1] // 128, 128)


def own_body(sizes, place, mine, out, target_t):
    out[...] = picked(*sizes, place, mine, target_t)


def dispatch_body(sizes, place, own, neighbour, outgoing):
    outgoing[:, 1 - place[SIDE]] = picked(*sizes, place, neighbour)
    outgoing[:, place[SIDE]] = own[...]


def gather_body(place, w_gate, w_up, one, two, three, weights, sems):
    both, cols = one.shape
    share = both // 2
    copies = copy_all(
        [
            (w.at[units_of(place, 0, share), :], weights.at[n * share : (n + 1) * share, :cols])
            for n, w in enumerate((w_gate, w_up))
        ],
        sems,
    )
    for shift, piece in enumerate((one, two, three), 1):
        weights[:, shift * cols : (shift + 1) * cols] = piece[...]
    for copy in copies:
        copy.wait()


def gate_up_body(mine, place, rows, weights, out):
    half = out.shape[0]
    for core in range(2):
        start = (core if mine else 1 - core) * (rows.shape[0] // 2)

        @pl.when(place[CORE] == core)
        def _():
            flat = rows[start : start + rows.shape[0] // 2].reshape(half, weights.shape[1])
            total = lax.dot_general(flat, weights[...], NT, preferred_element_type=jnp.float32)
            out[...] = total.astype(out.dtype)


def hidden_body(mine, theirs, hidden):
    units = hidden.shape[1]
    total = mine[...] + theirs[...].astype(jnp.float32)
    gate, up = total[:, :units], total[:, units:]
    hidden[...] = (gate / (1 + jnp.exp(-gate)) * up).astype(jnp.bfloat16)


def down(hidden, w_down):
    units = hidden.shape[2]
    total = functools.reduce(
        jnp.add,
        [
            jnp.dot(
                hidden[z], w_down[z * units : (z + 1) * units, :], preferred_element_type=jnp.float32
            )
            for z in range(CHIPS)
        ],
    )
    return total.astype(jnp.bfloat16)


def down_own_body(own, w_down, out):
    out[...] = down(own, w_down)


def down_body(place, own, other, w_down, out):
    blocks, cap = out.shape[:2]
    part = blocks // 4
    for value, which in ((own[...], place[CORE]), (down(other, w_down), 1 - place[CORE])):
        value = value.reshape(part, 2, cap, *out.shape[2:])
        for side in range(2):
            out[pl.ds(side * (blocks // 2) + which * part, part)] = value[:, side]


def combine_body(target_t, weight_t, returned, out):
    top, rows = target_t.shape
    slots = returned.shape[0] * returned.shape[1]
    slot_ids = lax.broadcasted_iota(jnp.int32, (slots, rows), 0)
    spread = jnp.zeros((slots, rows), jnp.float32)
    for k in range(top):
        spread += jnp.where(slot_ids == target_t[k : k + 1, :], weight_t[k : k + 1, :], 0.0)
    high = spread.astype(jnp.bfloat16)
    low = (spread - high.astype(jnp.float32)).astype(jnp.bfloat16)
    flat = returned[...].reshape(slots, out.shape[1])
    total = lax.dot_general(high, flat, TN, preferred_element_type=jnp.float32)
    total += lax.dot_general(low, flat, TN, preferred_element_type=jnp.float32)
    out[...] = total.astype(jnp.bfloat16)


def on_device(tokens, routes, route_weight, w_gate, w_up, w_down):
    tok_count, top = routes.shape
    _, units, cols = w_gate.shape
    side = lax.axis_size("plane")
    experts = 2 * side
    cap = max(2, (11 * tok_count + experts - 1) // experts)
    slots = experts * cap
    share = units // CHIPS
    half = slots // 2
    bf16 = jnp.bfloat16
    dma = pltpu.SemaphoreType.DMA
    swap = [(0, 1), (1, 0)]
    place = jnp.stack([lax.axis_index(a) for a in ("core", "chip", "side")]).astype(jnp.int32)

    part = jax.ShapeDtypeStruct((2 * share, cols), bf16)
    mine, two = call(
        first_body,
        (jax.ShapeDtypeStruct((tok_count + 16, CHIPS * cols), bf16),) + (part,),
        place,
        routes.T,
        tokens,
        w_gate[0],
        w_up[0],
        scalars=1,
        raw=4,
        scratch=[pltpu.VMEM((top, tok_count), jnp.int32), dma((3 + CHIPS,))],
    )
    neighbour = lax.ppermute(mine, "side", swap)
    sizes = (top, cap, experts, side)
    chunk = (cap, CHIPS * cols // 128, 128)
    picked_own, target_t = call(
        functools.partial(own_body, sizes),
        (
            jax.ShapeDtypeStruct((side, *chunk), bf16),
            jax.ShapeDtypeStruct((top, tok_count), jnp.int32),
        ),
        place,
        mine,
        scalars=1,
    )
    outgoing = call(
        functools.partial(dispatch_body, sizes),
        jax.ShapeDtypeStruct((side, 2, *chunk), bf16),
        place,
        picked_own,
        neighbour,
        scalars=1,
        flops=PICK,
    )
    received = lax.all_to_all(outgoing, "plane", split_axis=0, concat_axis=0, tiled=True)
    ring = [[(i, (i + shift) % CHIPS) for i in range(CHIPS)] for shift in range(CHIPS)]
    two = lax.ppermute(two, "chip", ring[2])
    one, three = call(
        pack_body,
        (part, part),
        place,
        w_gate[0],
        w_up[0],
        two,
        scalars=1,
        raw=2,
        scratch=[dma((4,))],
        flops=PACK,
    )
    pieces = [lax.ppermute(one, "chip", ring[1]), two, lax.ppermute(three, "chip", ring[3])]
    weights = call(
        gather_body,
        jax.ShapeDtypeStruct((2 * share, CHIPS * cols), bf16),
        place,
        w_gate[0],
        w_up[0],
        *pieces,
        scalars=1,
        raw=2,
        scratch=[dma((2,))],
    )
    theirs = call(
        functools.partial(gate_up_body, False),
        jax.ShapeDtypeStruct((half, 2 * share), bf16),
        place,
        received,
        weights,
        scalars=1,
    )
    theirs = lax.ppermute(theirs, "core", swap)
    mine = call(
        functools.partial(gate_up_body, True),
        jax.ShapeDtypeStruct((half, 2 * share), jnp.float32),
        place,
        received,
        weights,
        scalars=1,
    )
    hidden = call(hidden_body, jax.ShapeDtypeStruct((half, share), bf16), mine, theirs)
    own = lax.all_gather(hidden, "chip", axis=0)
    other = lax.ppermute(own, "core", swap)
    produced = call(
        down_body,
        jax.ShapeDtypeStruct((experts, cap, cols // 128, 128), bf16),
        place,
        call(down_own_body, jax.ShapeDtypeStruct((half, cols), bf16), own, w_down[0]),
        other,
        w_down[0],
        scalars=1,
    )
    returned = lax.all_to_all(produced, ("side", "plane"), split_axis=0, concat_axis=0, tiled=True)
    return call(
        combine_body,
        jax.ShapeDtypeStruct((tok_count, cols), bf16),
        target_t,
        route_weight.T,
        returned,
    )


def solution(mesh):
    fine = Mesh(
        mesh.devices.reshape(2, mesh.shape["wide"] // 2, CHIPS, 2), ("side", "plane", "chip", "core")
    )
    wide, narrow = ("side", "plane"), ("chip", "core")
    return jax.shard_map(
        on_device,
        mesh=fine,
        in_specs=(
            P(wide, None),
            P(wide, None),
            P(wide, None),
            P(wide, None, narrow),
            P(wide, None, narrow),
            P(wide, None, narrow),
        ),
        out_specs=P(wide, narrow),
        check_vma=False,
    )
```

```python
import functools

import jax
import jax.numpy as jnp
from jax import lax
from jax.experimental import pallas as pl
from jax.experimental.pallas import tpu as pltpu
from jax.sharding import Mesh
from jax.sharding import PartitionSpec as P

VMEM = pl.BlockSpec(memory_space=pltpu.VMEM)
HBM = pl.BlockSpec(memory_space=pltpu.HBM)
SMEM = pl.BlockSpec(memory_space=pltpu.SMEM)
NT = (((1,), (1,)), ((), ()))
TN = (((0,), (0,)), ((), ()))


HOLD = 30_000_000_000
PICK = 10_000_000_000
CHIPS = 4
CORE, CHIP, SIDE = range(3)


def call(body, outs, *operands, scalars=0, raw=0, scratch=(), flops=None, out_space=VMEM):
    operands = list(operands)
    for n in range(scalars, scalars + raw):
        operands[n] = pltpu.with_memory_space_constraint(operands[n], pltpu.HBM)
    cost = None if flops is None else pl.CostEstimate(flops=flops, transcendentals=0, bytes_accessed=0)
    return pl.pallas_call(
        body,
        out_shape=outs,
        in_specs=[SMEM] * scalars + [HBM] * raw + [VMEM] * (len(operands) - scalars - raw),
        out_specs=jax.tree.map(lambda _: out_space, outs),
        scratch_shapes=scratch,
        cost_estimate=cost,
        compiler_params=pltpu.CompilerParams(vmem_limit_bytes=16 << 20),
    )(*operands)


def copy_all(pairs, sems):
    copies = [pltpu.make_async_copy(src, dst, sems.at[n]) for n, (src, dst) in enumerate(pairs)]
    for copy in copies:
        copy.start()
    return copies


def units_of(place, shift, share):
    start = lax.rem(place[CHIP] + shift, CHIPS) * share
    return pl.ds(pl.multiple_of(start, 16), share)


def first_body(place, routes_hbm, tokens_hbm, w_gate, w_up, mine, *refs):
    *pieces, routes_t, sems = refs
    top, rows = routes_t.shape
    cols = mine.shape[1] // CHIPS
    share = pieces[0].shape[0] // 2
    pairs = [(routes_hbm, routes_t)]
    for shift in range(CHIPS):
        block = lax.rem(place[CHIP] - shift + CHIPS, CHIPS) * 2 + place[CORE]
        columns = pl.ds(pl.multiple_of(block * cols, cols), cols)
        pairs.append((tokens_hbm.at[:, columns], mine.at[:rows, shift * cols : (shift + 1) * cols]))
    for shift, out in enumerate(pieces, 1):
        pairs.append((w_gate.at[units_of(place, shift, share), :], out.at[:share, :]))
        pairs.append((w_up.at[units_of(place, shift, share), :], out.at[share:, :]))
    copies = copy_all(pairs, sems)
    mine[rows:, :] = jnp.zeros((mine.shape[0] - rows, mine.shape[1]), mine.dtype)
    copies[0].wait()
    mine[rows : rows + top, :rows] = routes_t[...].astype(mine.dtype)
    for copy in copies[1:]:
        copy.wait()


def hold_body(place, w_gate, w_up, one, three, _, here, one_out, three_out, sems):
    share = here.shape[0] // 2
    pairs = [
        (w.at[units_of(place, 0, share), :], here.at[n * share : (n + 1) * share, :])
        for n, w in enumerate((w_gate, w_up))
    ]
    copies = copy_all(pairs, sems)
    one_out[...] = one[...]
    three_out[...] = three[...]
    for copy in copies:
        copy.wait()


def picked(top, cap, experts, side, place, block, target_t=None):
    rows = block.shape[0] - 16
    slots = side * cap
    routes_t = block[rows:, :rows].astype(jnp.float32).astype(jnp.int32)
    expert_ids = lax.broadcasted_iota(jnp.int32, (experts, rows), 0)
    chosen = [(routes_t[k : k + 1, :] == expert_ids).astype(jnp.float32) for k in range(top)]
    named = functools.reduce(jnp.add, chosen)
    earlier = (
        lax.broadcasted_iota(jnp.int32, (rows, rows), 0) < lax.broadcasted_iota(jnp.int32, (rows, rows), 1)
    ).astype(jnp.bfloat16)
    before = jnp.dot(named.astype(jnp.bfloat16), earlier, preferred_element_type=jnp.float32)
    slot_ids = lax.broadcasted_iota(jnp.int32, (slots, rows), 0)
    picker = jnp.zeros((slots, rows), jnp.float32)
    for k in range(top):
        slot = jnp.sum(chosen[k] * before, axis=0, keepdims=True).astype(jnp.int32)
        target = routes_t[k : k + 1, :] * cap + slot
        if target_t is not None:
            target_t[k : k + 1, :] = target
        picker += (slot_ids == target - place[SIDE] * slots).astype(jnp.float32)
    rows_out = jnp.dot(picker.astype(jnp.bfloat16), block[:rows, :], preferred_element_type=jnp.float32)
    return rows_out.astype(jnp.bfloat16).reshape(side, cap, block.shape[1] // 128, 128)


def own_body(sizes, place, mine, out, target_t):
    out[...] = picked(*sizes, place, mine, target_t)


def dispatch_body(sizes, place, own, neighbour, outgoing):
    outgoing[:, 1 - place[SIDE]] = picked(*sizes, place, neighbour)
    outgoing[:, place[SIDE]] = own[...]


def gate_up_body(mine, place, rows, *refs):
    *weights, out = refs
    half, cols = out.shape[0], weights[0].shape[1]
    for core in range(2):
        start = (core if mine else 1 - core) * (rows.shape[0] // 2)

        @pl.when(place[CORE] == core)
        def _():
            flat = rows[start : start + rows.shape[0] // 2].reshape(half, CHIPS * cols)
            total = functools.reduce(
                jnp.add,
                [
                    lax.dot_general(
                        flat[:, n * cols : (n + 1) * cols], w[...], NT, preferred_element_type=jnp.float32
                    )
                    for n, w in enumerate(weights)
                ],
            )
            out[...] = total.astype(out.dtype)


def hidden_body(mine, theirs, hidden):
    units = hidden.shape[1]
    total = mine[...] + theirs[...].astype(jnp.float32)
    gate, up = total[:, :units], total[:, units:]
    hidden[...] = (gate / (1 + jnp.exp(-gate)) * up).astype(jnp.bfloat16)


def down(hidden, w_down):
    units = hidden.shape[2]
    total = functools.reduce(
        jnp.add,
        [
            jnp.dot(
                hidden[z], w_down[z * units : (z + 1) * units, :], preferred_element_type=jnp.float32
            )
            for z in range(CHIPS)
        ],
    )
    return total.astype(jnp.bfloat16)


def down_own_body(own, w_down, out):
    out[...] = down(own, w_down)


def down_body(place, own, other, w_down, out):
    blocks, cap = out.shape[:2]
    part = blocks // 4
    for value, which in ((own[...], place[CORE]), (down(other, w_down), 1 - place[CORE])):
        value = value.reshape(part, 2, cap, *out.shape[2:])
        for side in range(2):
            out[pl.ds(side * (blocks // 2) + which * part, part)] = value[:, side]


def combine_body(target_t, weight_t, returned, out):
    top, rows = target_t.shape
    slots = returned.shape[0] * returned.shape[1]
    slot_ids = lax.broadcasted_iota(jnp.int32, (slots, rows), 0)
    spread = jnp.zeros((slots, rows), jnp.float32)
    for k in range(top):
        spread += jnp.where(slot_ids == target_t[k : k + 1, :], weight_t[k : k + 1, :], 0.0)
    high = spread.astype(jnp.bfloat16)
    low = (spread - high.astype(jnp.float32)).astype(jnp.bfloat16)
    flat = returned[...].reshape(slots, out.shape[1])
    total = lax.dot_general(high, flat, TN, preferred_element_type=jnp.float32)
    total += lax.dot_general(low, flat, TN, preferred_element_type=jnp.float32)
    out[...] = total.astype(jnp.bfloat16)


def on_device(tokens, routes, route_weight, w_gate, w_up, w_down):
    tok_count, top = routes.shape
    _, units, cols = w_gate.shape
    side = lax.axis_size("plane")
    experts = 2 * side
    cap = max(2, (11 * tok_count + experts - 1) // experts)
    slots = experts * cap
    share = units // CHIPS
    half = slots // 2
    bf16 = jnp.bfloat16
    dma = pltpu.SemaphoreType.DMA
    swap = [(0, 1), (1, 0)]
    place = jnp.stack([lax.axis_index(a) for a in ("core", "chip", "side")]).astype(jnp.int32)

    part = jax.ShapeDtypeStruct((2 * share, cols), bf16)
    mine, one, two, three = call(
        first_body,
        (jax.ShapeDtypeStruct((tok_count + 16, CHIPS * cols), bf16),) + (part,) * (CHIPS - 1),
        place,
        routes.T,
        tokens,
        w_gate[0],
        w_up[0],
        scalars=1,
        raw=4,
        scratch=[pltpu.VMEM((top, tok_count), jnp.int32), dma((3 * CHIPS - 1,))],
    )
    neighbour = lax.ppermute(mine, "side", swap)
    sizes = (top, cap, experts, side)
    chunk = (cap, CHIPS * cols // 128, 128)
    picked_own, target_t = call(
        functools.partial(own_body, sizes),
        (
            jax.ShapeDtypeStruct((side, *chunk), bf16),
            jax.ShapeDtypeStruct((top, tok_count), jnp.int32),
        ),
        place,
        mine,
        scalars=1,
    )
    outgoing = call(
        functools.partial(dispatch_body, sizes),
        jax.ShapeDtypeStruct((side, 2, *chunk), bf16),
        place,
        picked_own,
        neighbour,
        scalars=1,
        flops=PICK,
    )
    received = lax.all_to_all(outgoing, "plane", split_axis=0, concat_axis=0, tiled=True)
    ring = [[(i, (i + shift) % CHIPS) for i in range(CHIPS)] for shift in range(CHIPS)]
    two = lax.ppermute(two, "chip", ring[2])
    here, one, three = call(
        hold_body,
        (part,) * 3,
        place,
        w_gate[0],
        w_up[0],
        one,
        three,
        two,
        scalars=1,
        raw=2,
        scratch=[dma((2,))],
        flops=HOLD,
    )
    one = lax.ppermute(one, "chip", ring[1])
    three = lax.ppermute(three, "chip", ring[3])
    weights = (here, one, two, three)
    theirs = call(
        functools.partial(gate_up_body, False),
        jax.ShapeDtypeStruct((half, 2 * share), bf16),
        place,
        received,
        *weights,
        scalars=1,
    )
    theirs = lax.ppermute(theirs, "core", swap)
    mine = call(
        functools.partial(gate_up_body, True),
        jax.ShapeDtypeStruct((half, 2 * share), jnp.float32),
        place,
        received,
        *weights,
        scalars=1,
    )
    hidden = call(hidden_body, jax.ShapeDtypeStruct((half, share), bf16), mine, theirs)
    own = lax.all_gather(hidden, "chip", axis=0)
    other = lax.ppermute(own, "core", swap)
    produced = call(
        down_body,
        jax.ShapeDtypeStruct((experts, cap, cols // 128, 128), bf16),
        place,
        call(down_own_body, jax.ShapeDtypeStruct((half, cols), bf16), own, w_down[0]),
        other,
        w_down[0],
        scalars=1,
    )
    returned = lax.all_to_all(produced, ("side", "plane"), split_axis=0, concat_axis=0, tiled=True)
    return call(
        combine_body,
        jax.ShapeDtypeStruct((tok_count, cols), bf16),
        target_t,
        route_weight.T,
        returned,
    )


def solution(mesh):
    fine = Mesh(
        mesh.devices.reshape(2, mesh.shape["wide"] // 2, CHIPS, 2), ("side", "plane", "chip", "core")
    )
    wide, narrow = ("side", "plane"), ("chip", "core")
    return jax.shard_map(
        on_device,
        mesh=fine,
        in_specs=(
            P(wide, None),
            P(wide, None),
            P(wide, None),
            P(wide, None, narrow),
            P(wide, None, narrow),
            P(wide, None, narrow),
        ),
        out_specs=P(wide, narrow),
        check_vma=False,
    )
```

```python
import functools

import jax
import jax.numpy as jnp
from jax import lax
from jax.experimental import pallas as pl
from jax.experimental.pallas import tpu as pltpu
from jax.sharding import Mesh
from jax.sharding import PartitionSpec as P

VMEM = pl.BlockSpec(memory_space=pltpu.VMEM)
HBM = pl.BlockSpec(memory_space=pltpu.HBM)
SMEM = pl.BlockSpec(memory_space=pltpu.SMEM)
NT = (((1,), (1,)), ((), ()))
TN = (((0,), (0,)), ((), ()))


HOLD = 30_000_000_000
PICK = 10_000_000_000
CHIPS = 4
CORE, CHIP, SIDE = range(3)


def call(body, outs, *operands, scalars=0, raw=0, scratch=(), flops=None, out_space=VMEM):
    operands = list(operands)
    for n in range(scalars, scalars + raw):
        operands[n] = pltpu.with_memory_space_constraint(operands[n], pltpu.HBM)
    cost = None if flops is None else pl.CostEstimate(flops=flops, transcendentals=0, bytes_accessed=0)
    return pl.pallas_call(
        body,
        out_shape=outs,
        in_specs=[SMEM] * scalars + [HBM] * raw + [VMEM] * (len(operands) - scalars - raw),
        out_specs=jax.tree.map(lambda _: out_space, outs),
        scratch_shapes=scratch,
        cost_estimate=cost,
        compiler_params=pltpu.CompilerParams(vmem_limit_bytes=16 << 20),
    )(*operands)


def copy_all(pairs, sems):
    copies = [pltpu.make_async_copy(src, dst, sems.at[n]) for n, (src, dst) in enumerate(pairs)]
    for copy in copies:
        copy.start()
    return copies


def units_of(place, shift, share):
    start = lax.rem(place[CHIP] + shift, CHIPS) * share
    return pl.ds(pl.multiple_of(start, 16), share)


def first_body(place, routes_hbm, tokens_hbm, w_gate, w_up, mine, *refs):
    *pieces, routes_t, sems = refs
    top, rows = routes_t.shape
    cols = mine.shape[1] // CHIPS
    share = pieces[0].shape[0] // 2
    pairs = [(routes_hbm, routes_t)]
    for shift in range(CHIPS):
        block = lax.rem(place[CHIP] - shift + CHIPS, CHIPS) * 2 + place[CORE]
        columns = pl.ds(pl.multiple_of(block * cols, cols), cols)
        pairs.append((tokens_hbm.at[:, columns], mine.at[:rows, shift * cols : (shift + 1) * cols]))
    for shift, out in enumerate(pieces, 1):
        pairs.append((w_gate.at[units_of(place, shift, share), :], out.at[:share, :]))
        pairs.append((w_up.at[units_of(place, shift, share), :], out.at[share:, :]))
    copies = copy_all(pairs, sems)
    mine[rows:, :] = jnp.zeros((mine.shape[0] - rows, mine.shape[1]), mine.dtype)
    copies[0].wait()
    mine[rows : rows + top, :rows] = routes_t[...].astype(mine.dtype)
    for copy in copies[1:]:
        copy.wait()


def hold_body(place, w_gate, w_up, two, three, _, here, two_out, three_out, sems):
    share = here.shape[0] // 2
    pairs = [
        (w.at[units_of(place, 0, share), :], here.at[n * share : (n + 1) * share, :])
        for n, w in enumerate((w_gate, w_up))
    ]
    copies = copy_all(pairs, sems)
    two_out[...] = two[...]
    three_out[...] = three[...]
    for copy in copies:
        copy.wait()


def picked(top, cap, experts, side, place, block, target_t=None):
    rows = block.shape[0] - 16
    slots = side * cap
    routes_t = block[rows:, :rows].astype(jnp.float32).astype(jnp.int32)
    expert_ids = lax.broadcasted_iota(jnp.int32, (experts, rows), 0)
    chosen = [(routes_t[k : k + 1, :] == expert_ids).astype(jnp.float32) for k in range(top)]
    named = functools.reduce(jnp.add, chosen)
    earlier = (
        lax.broadcasted_iota(jnp.int32, (rows, rows), 0) < lax.broadcasted_iota(jnp.int32, (rows, rows), 1)
    ).astype(jnp.bfloat16)
    before = jnp.dot(named.astype(jnp.bfloat16), earlier, preferred_element_type=jnp.float32)
    slot_ids = lax.broadcasted_iota(jnp.int32, (slots, rows), 0)
    picker = jnp.zeros((slots, rows), jnp.float32)
    for k in range(top):
        slot = jnp.sum(chosen[k] * before, axis=0, keepdims=True).astype(jnp.int32)
        target = routes_t[k : k + 1, :] * cap + slot
        if target_t is not None:
            target_t[k : k + 1, :] = target
        picker += (slot_ids == target - place[SIDE] * slots).astype(jnp.float32)
    rows_out = jnp.dot(picker.astype(jnp.bfloat16), block[:rows, :], preferred_element_type=jnp.float32)
    return rows_out.astype(jnp.bfloat16).reshape(side, cap, block.shape[1] // 128, 128)


def own_body(sizes, place, mine, out, target_t):
    out[...] = picked(*sizes, place, mine, target_t)


def dispatch_body(sizes, place, own, neighbour, outgoing):
    outgoing[:, 1 - place[SIDE]] = picked(*sizes, place, neighbour)
    outgoing[:, place[SIDE]] = own[...]


def gate_up_body(mine, place, rows, *refs):
    *weights, out = refs
    half, cols = out.shape[0], weights[0].shape[1]
    for core in range(2):
        start = (core if mine else 1 - core) * (rows.shape[0] // 2)

        @pl.when(place[CORE] == core)
        def _():
            flat = rows[start : start + rows.shape[0] // 2].reshape(half, CHIPS * cols)
            total = functools.reduce(
                jnp.add,
                [
                    lax.dot_general(
                        flat[:, n * cols : (n + 1) * cols], w[...], NT, preferred_element_type=jnp.float32
                    )
                    for n, w in enumerate(weights)
                ],
            )
            out[...] = total.astype(out.dtype)


def hidden_body(mine, theirs, hidden):
    units = hidden.shape[1]
    total = mine[...] + theirs[...].astype(jnp.float32)
    gate, up = total[:, :units], total[:, units:]
    hidden[...] = (gate / (1 + jnp.exp(-gate)) * up).astype(jnp.bfloat16)


def down(hidden, w_down):
    units = hidden.shape[2]
    total = functools.reduce(
        jnp.add,
        [
            jnp.dot(
                hidden[z], w_down[z * units : (z + 1) * units, :], preferred_element_type=jnp.float32
            )
            for z in range(CHIPS)
        ],
    )
    return total.astype(jnp.bfloat16)


def down_own_body(own, w_down, out):
    out[...] = down(own, w_down)


def down_body(place, own, other, w_down, out):
    blocks, cap = out.shape[:2]
    part = blocks // 4
    for value, which in ((own[...], place[CORE]), (down(other, w_down), 1 - place[CORE])):
        value = value.reshape(part, 2, cap, *out.shape[2:])
        for side in range(2):
            out[pl.ds(side * (blocks // 2) + which * part, part)] = value[:, side]


def combine_body(target_t, weight_t, returned, out):
    top, rows = target_t.shape
    slots = returned.shape[0] * returned.shape[1]
    slot_ids = lax.broadcasted_iota(jnp.int32, (slots, rows), 0)
    spread = jnp.zeros((slots, rows), jnp.float32)
    for k in range(top):
        spread += jnp.where(slot_ids == target_t[k : k + 1, :], weight_t[k : k + 1, :], 0.0)
    high = spread.astype(jnp.bfloat16)
    low = (spread - high.astype(jnp.float32)).astype(jnp.bfloat16)
    flat = returned[...].reshape(slots, out.shape[1])
    total = lax.dot_general(high, flat, TN, preferred_element_type=jnp.float32)
    total += lax.dot_general(low, flat, TN, preferred_element_type=jnp.float32)
    out[...] = total.astype(jnp.bfloat16)


def on_device(tokens, routes, route_weight, w_gate, w_up, w_down):
    tok_count, top = routes.shape
    _, units, cols = w_gate.shape
    side = lax.axis_size("plane")
    experts = 2 * side
    cap = max(2, (11 * tok_count + experts - 1) // experts)
    slots = experts * cap
    share = units // CHIPS
    half = slots // 2
    bf16 = jnp.bfloat16
    dma = pltpu.SemaphoreType.DMA
    swap = [(0, 1), (1, 0)]
    place = jnp.stack([lax.axis_index(a) for a in ("core", "chip", "side")]).astype(jnp.int32)

    part = jax.ShapeDtypeStruct((2 * share, cols), bf16)
    mine, one, two, three = call(
        first_body,
        (jax.ShapeDtypeStruct((tok_count + 16, CHIPS * cols), bf16),) + (part,) * (CHIPS - 1),
        place,
        routes.T,
        tokens,
        w_gate[0],
        w_up[0],
        scalars=1,
        raw=4,
        scratch=[pltpu.VMEM((top, tok_count), jnp.int32), dma((3 * CHIPS - 1,))],
    )
    neighbour = lax.ppermute(mine, "side", swap)
    sizes = (top, cap, experts, side)
    chunk = (cap, CHIPS * cols // 128, 128)
    picked_own, target_t = call(
        functools.partial(own_body, sizes),
        (
            jax.ShapeDtypeStruct((side, *chunk), bf16),
            jax.ShapeDtypeStruct((top, tok_count), jnp.int32),
        ),
        place,
        mine,
        scalars=1,
    )
    outgoing = call(
        functools.partial(dispatch_body, sizes),
        jax.ShapeDtypeStruct((side, 2, *chunk), bf16),
        place,
        picked_own,
        neighbour,
        scalars=1,
        flops=PICK,
    )
    received = lax.all_to_all(outgoing, "plane", split_axis=0, concat_axis=0, tiled=True)
    ring = [[(i, (i + shift) % CHIPS) for i in range(CHIPS)] for shift in range(CHIPS)]
    one = lax.ppermute(one, "chip", ring[1])
    here, two, three = call(
        hold_body,
        (part,) * 3,
        place,
        w_gate[0],
        w_up[0],
        two,
        three,
        one,
        scalars=1,
        raw=2,
        scratch=[dma((2,))],
        flops=HOLD,
    )
    two = lax.ppermute(two, "chip", ring[2])
    three = lax.ppermute(three, "chip", ring[3])
    weights = (here, one, two, three)
    theirs = call(
        functools.partial(gate_up_body, False),
        jax.ShapeDtypeStruct((half, 2 * share), bf16),
        place,
        received,
        *weights,
        scalars=1,
    )
    theirs = lax.ppermute(theirs, "core", swap)
    mine = call(
        functools.partial(gate_up_body, True),
        jax.ShapeDtypeStruct((half, 2 * share), jnp.float32),
        place,
        received,
        *weights,
        scalars=1,
    )
    hidden = call(hidden_body, jax.ShapeDtypeStruct((half, share), bf16), mine, theirs)
    own = lax.all_gather(hidden, "chip", axis=0)
    other = lax.ppermute(own, "core", swap)
    produced = call(
        down_body,
        jax.ShapeDtypeStruct((experts, cap, cols // 128, 128), bf16),
        place,
        call(down_own_body, jax.ShapeDtypeStruct((half, cols), bf16), own, w_down[0]),
        other,
        w_down[0],
        scalars=1,
    )
    returned = lax.all_to_all(produced, ("side", "plane"), split_axis=0, concat_axis=0, tiled=True)
    return call(
        combine_body,
        jax.ShapeDtypeStruct((tok_count, cols), bf16),
        target_t,
        route_weight.T,
        returned,
    )


def solution(mesh):
    fine = Mesh(
        mesh.devices.reshape(2, mesh.shape["wide"] // 2, CHIPS, 2), ("side", "plane", "chip", "core")
    )
    wide, narrow = ("side", "plane"), ("chip", "core")
    return jax.shard_map(
        on_device,
        mesh=fine,
        in_specs=(
            P(wide, None),
            P(wide, None),
            P(wide, None),
            P(wide, None, narrow),
            P(wide, None, narrow),
            P(wide, None, narrow),
        ),
        out_specs=P(wide, narrow),
        check_vma=False,
    )
```

```python
import functools

import jax
import jax.numpy as jnp
from jax import lax
from jax.experimental import pallas as pl
from jax.experimental.pallas import tpu as pltpu
from jax.sharding import Mesh
from jax.sharding import PartitionSpec as P

VMEM = pl.BlockSpec(memory_space=pltpu.VMEM)
HBM = pl.BlockSpec(memory_space=pltpu.HBM)
SMEM = pl.BlockSpec(memory_space=pltpu.SMEM)
NT = (((1,), (1,)), ((), ()))
TN = (((0,), (0,)), ((), ()))


HOLD = 30_000_000_000
CHIPS = 4
CORE, CHIP, SIDE = range(3)


def call(body, outs, *operands, scalars=0, raw=0, scratch=(), flops=None, out_space=VMEM):
    operands = list(operands)
    for n in range(scalars, scalars + raw):
        operands[n] = pltpu.with_memory_space_constraint(operands[n], pltpu.HBM)
    cost = None if flops is None else pl.CostEstimate(flops=flops, transcendentals=0, bytes_accessed=0)
    return pl.pallas_call(
        body,
        out_shape=outs,
        in_specs=[SMEM] * scalars + [HBM] * raw + [VMEM] * (len(operands) - scalars - raw),
        out_specs=jax.tree.map(lambda _: out_space, outs),
        scratch_shapes=scratch,
        cost_estimate=cost,
        compiler_params=pltpu.CompilerParams(vmem_limit_bytes=16 << 20),
    )(*operands)


def copy_all(pairs, sems):
    copies = [pltpu.make_async_copy(src, dst, sems.at[n]) for n, (src, dst) in enumerate(pairs)]
    for copy in copies:
        copy.start()
    return copies


def units_of(place, shift, share):
    start = lax.rem(place[CHIP] + shift, CHIPS) * share
    return pl.ds(pl.multiple_of(start, 16), share)


def first_body(place, routes_hbm, tokens_hbm, w_gate, w_up, mine, *refs):
    *pieces, routes_t, sems = refs
    top, rows = routes_t.shape
    cols = mine.shape[1] // CHIPS
    share = pieces[0].shape[0] // 2
    pairs = [(routes_hbm, routes_t)]
    for shift in range(CHIPS):
        block = lax.rem(place[CHIP] - shift + CHIPS, CHIPS) * 2 + place[CORE]
        columns = pl.ds(pl.multiple_of(block * cols, cols), cols)
        pairs.append((tokens_hbm.at[:, columns], mine.at[:rows, shift * cols : (shift + 1) * cols]))
    for shift, out in zip((1, 3), pieces):
        pairs.append((w_gate.at[units_of(place, shift, share), :], out.at[:share, :]))
        pairs.append((w_up.at[units_of(place, shift, share), :], out.at[share:, :]))
    copies = copy_all(pairs, sems)
    mine[rows:, :] = jnp.zeros((mine.shape[0] - rows, mine.shape[1]), mine.dtype)
    copies[0].wait()
    mine[rows : rows + top, :rows] = routes_t[...].astype(mine.dtype)
    for copy in copies[1:]:
        copy.wait()


def hold_body(place, w_gate, w_up, one, three, _, here, one_out, three_out, sems):
    share = here.shape[0] // 2
    pairs = [
        (w.at[units_of(place, 0, share), :], here.at[n * share : (n + 1) * share, :])
        for n, w in enumerate((w_gate, w_up))
    ]
    copies = copy_all(pairs, sems)
    one_out[...] = one[...]
    three_out[...] = three[...]
    for copy in copies:
        copy.wait()


def picked(top, cap, experts, side, place, block, target_t=None):
    rows = block.shape[0] - 16
    slots = side * cap
    routes_t = block[rows:, :rows].astype(jnp.float32).astype(jnp.int32)
    expert_ids = lax.broadcasted_iota(jnp.int32, (experts, rows), 0)
    chosen = [(routes_t[k : k + 1, :] == expert_ids).astype(jnp.float32) for k in range(top)]
    named = functools.reduce(jnp.add, chosen)
    earlier = (
        lax.broadcasted_iota(jnp.int32, (rows, rows), 0) < lax.broadcasted_iota(jnp.int32, (rows, rows), 1)
    ).astype(jnp.bfloat16)
    before = jnp.dot(named.astype(jnp.bfloat16), earlier, preferred_element_type=jnp.float32)
    slot_ids = lax.broadcasted_iota(jnp.int32, (slots, rows), 0)
    picker = jnp.zeros((slots, rows), jnp.float32)
    for k in range(top):
        slot = jnp.sum(chosen[k] * before, axis=0, keepdims=True).astype(jnp.int32)
        target = routes_t[k : k + 1, :] * cap + slot
        if target_t is not None:
            target_t[k : k + 1, :] = target
        picker += (slot_ids == target - place[SIDE] * slots).astype(jnp.float32)
    rows_out = jnp.dot(picker.astype(jnp.bfloat16), block[:rows, :], preferred_element_type=jnp.float32)
    return rows_out.astype(jnp.bfloat16).reshape(side, cap, block.shape[1] // 128, 128)


def own_body(sizes, place, mine, out, target_t):
    out[...] = picked(*sizes, place, mine, target_t)


def dispatch_body(sizes, place, w_gate, w_up, own, neighbour, outgoing, two, sems):
    share = two.shape[0] // 2
    pairs = [
        (w.at[units_of(place, 2, share), :], two.at[n * share : (n + 1) * share, :])
        for n, w in enumerate((w_gate, w_up))
    ]
    copies = copy_all(pairs, sems)
    outgoing[:, 1 - place[SIDE]] = picked(*sizes, place, neighbour)
    outgoing[:, place[SIDE]] = own[...]
    for copy in copies:
        copy.wait()


def gate_up_body(mine, place, rows, *refs):
    *weights, out = refs
    half, cols = out.shape[0], weights[0].shape[1]
    for core in range(2):
        start = (core if mine else 1 - core) * (rows.shape[0] // 2)

        @pl.when(place[CORE] == core)
        def _():
            flat = rows[start : start + rows.shape[0] // 2].reshape(half, CHIPS * cols)
            total = functools.reduce(
                jnp.add,
                [
                    lax.dot_general(
                        flat[:, n * cols : (n + 1) * cols], w[...], NT, preferred_element_type=jnp.float32
                    )
                    for n, w in enumerate(weights)
                ],
            )
            out[...] = total.astype(out.dtype)


def hidden_body(mine, theirs, hidden):
    units = hidden.shape[1]
    total = mine[...] + theirs[...].astype(jnp.float32)
    gate, up = total[:, :units], total[:, units:]
    hidden[...] = (gate / (1 + jnp.exp(-gate)) * up).astype(jnp.bfloat16)


def down(hidden, w_down):
    units = hidden.shape[2]
    total = functools.reduce(
        jnp.add,
        [
            jnp.dot(
                hidden[z], w_down[z * units : (z + 1) * units, :], preferred_element_type=jnp.float32
            )
            for z in range(CHIPS)
        ],
    )
    return total.astype(jnp.bfloat16)


def down_own_body(own, w_down, out):
    out[...] = down(own, w_down)


def down_body(place, own, other, w_down, out):
    blocks, cap = out.shape[:2]
    part = blocks // 4
    for value, which in ((own[...], place[CORE]), (down(other, w_down), 1 - place[CORE])):
        value = value.reshape(part, 2, cap, *out.shape[2:])
        for side in range(2):
            out[pl.ds(side * (blocks // 2) + which * part, part)] = value[:, side]


def combine_body(target_t, weight_t, returned, out):
    top, rows = target_t.shape
    slots = returned.shape[0] * returned.shape[1]
    slot_ids = lax.broadcasted_iota(jnp.int32, (slots, rows), 0)
    spread = jnp.zeros((slots, rows), jnp.float32)
    for k in range(top):
        spread += jnp.where(slot_ids == target_t[k : k + 1, :], weight_t[k : k + 1, :], 0.0)
    high = spread.astype(jnp.bfloat16)
    low = (spread - high.astype(jnp.float32)).astype(jnp.bfloat16)
    flat = returned[...].reshape(slots, out.shape[1])
    total = lax.dot_general(high, flat, TN, preferred_element_type=jnp.float32)
    total += lax.dot_general(low, flat, TN, preferred_element_type=jnp.float32)
    out[...] = total.astype(jnp.bfloat16)


def on_device(tokens, routes, route_weight, w_gate, w_up, w_down):
    tok_count, top = routes.shape
    _, units, cols = w_gate.shape
    side = lax.axis_size("plane")
    experts = 2 * side
    cap = max(2, (11 * tok_count + experts - 1) // experts)
    slots = experts * cap
    share = units // CHIPS
    half = slots // 2
    bf16 = jnp.bfloat16
    dma = pltpu.SemaphoreType.DMA
    swap = [(0, 1), (1, 0)]
    place = jnp.stack([lax.axis_index(a) for a in ("core", "chip", "side")]).astype(jnp.int32)

    part = jax.ShapeDtypeStruct((2 * share, cols), bf16)
    mine, one, three = call(
        first_body,
        (jax.ShapeDtypeStruct((tok_count + 16, CHIPS * cols), bf16),) + (part,) * 2,
        place,
        routes.T,
        tokens,
        w_gate[0],
        w_up[0],
        scalars=1,
        raw=4,
        scratch=[pltpu.VMEM((top, tok_count), jnp.int32), dma((CHIPS + 5,))],
    )
    neighbour = lax.ppermute(mine, "side", swap)
    sizes = (top, cap, experts, side)
    chunk = (cap, CHIPS * cols // 128, 128)
    picked_own, target_t = call(
        functools.partial(own_body, sizes),
        (
            jax.ShapeDtypeStruct((side, *chunk), bf16),
            jax.ShapeDtypeStruct((top, tok_count), jnp.int32),
        ),
        place,
        mine,
        scalars=1,
    )
    outgoing, two = call(
        functools.partial(dispatch_body, sizes),
        (jax.ShapeDtypeStruct((side, 2, *chunk), bf16), part),
        place,
        w_gate[0],
        w_up[0],
        picked_own,
        neighbour,
        scalars=1,
        raw=2,
        scratch=[dma((2,))],
    )
    received = lax.all_to_all(outgoing, "plane", split_axis=0, concat_axis=0, tiled=True)
    ring = [[(i, (i + shift) % CHIPS) for i in range(CHIPS)] for shift in range(CHIPS)]
    two = lax.ppermute(two, "chip", ring[2])
    here, one, three = call(
        hold_body,
        (part,) * 3,
        place,
        w_gate[0],
        w_up[0],
        one,
        three,
        two,
        scalars=1,
        raw=2,
        scratch=[dma((2,))],
        flops=HOLD,
    )
    one = lax.ppermute(one, "chip", ring[1])
    three = lax.ppermute(three, "chip", ring[3])
    weights = (here, one, two, three)
    theirs = call(
        functools.partial(gate_up_body, False),
        jax.ShapeDtypeStruct((half, 2 * share), bf16),
        place,
        received,
        *weights,
        scalars=1,
    )
    theirs = lax.ppermute(theirs, "core", swap)
    mine = call(
        functools.partial(gate_up_body, True),
        jax.ShapeDtypeStruct((half, 2 * share), jnp.float32),
        place,
        received,
        *weights,
        scalars=1,
    )
    hidden = call(hidden_body, jax.ShapeDtypeStruct((half, share), bf16), mine, theirs)
    own = lax.all_gather(hidden, "chip", axis=0)
    other = lax.ppermute(own, "core", swap)
    produced = call(
        down_body,
        jax.ShapeDtypeStruct((experts, cap, cols // 128, 128), bf16),
        place,
        call(down_own_body, jax.ShapeDtypeStruct((half, cols), bf16), own, w_down[0]),
        other,
        w_down[0],
        scalars=1,
    )
    returned = lax.all_to_all(produced, ("side", "plane"), split_axis=0, concat_axis=0, tiled=True)
    return call(
        combine_body,
        jax.ShapeDtypeStruct((tok_count, cols), bf16),
        target_t,
        route_weight.T,
        returned,
    )


def solution(mesh):
    fine = Mesh(
        mesh.devices.reshape(2, mesh.shape["wide"] // 2, CHIPS, 2), ("side", "plane", "chip", "core")
    )
    wide, narrow = ("side", "plane"), ("chip", "core")
    return jax.shard_map(
        on_device,
        mesh=fine,
        in_specs=(
            P(wide, None),
            P(wide, None),
            P(wide, None),
            P(wide, None, narrow),
            P(wide, None, narrow),
            P(wide, None, narrow),
        ),
        out_specs=P(wide, narrow),
        check_vma=False,
    )
```

```python
import functools

import jax
import jax.numpy as jnp
from jax import lax
from jax.experimental import pallas as pl
from jax.experimental.pallas import tpu as pltpu
from jax.sharding import Mesh
from jax.sharding import PartitionSpec as P

VMEM = pl.BlockSpec(memory_space=pltpu.VMEM)
HBM = pl.BlockSpec(memory_space=pltpu.HBM)
SMEM = pl.BlockSpec(memory_space=pltpu.SMEM)
NT = (((1,), (1,)), ((), ()))
TN = (((0,), (0,)), ((), ()))


HOLD = 30_000_000_000
PICK = 10_000_000_000
CHIPS = 4
GROUPS = 4
CORE, CHIP, SIDE = range(3)


def call(body, outs, *operands, scalars=0, raw=0, scratch=(), flops=None, out_space=VMEM):
    operands = list(operands)
    for n in range(scalars, scalars + raw):
        operands[n] = pltpu.with_memory_space_constraint(operands[n], pltpu.HBM)
    cost = None if flops is None else pl.CostEstimate(flops=flops, transcendentals=0, bytes_accessed=0)
    return pl.pallas_call(
        body,
        out_shape=outs,
        in_specs=[SMEM] * scalars + [HBM] * raw + [VMEM] * (len(operands) - scalars - raw),
        out_specs=jax.tree.map(lambda _: out_space, outs),
        scratch_shapes=scratch,
        cost_estimate=cost,
        compiler_params=pltpu.CompilerParams(vmem_limit_bytes=16 << 20),
    )(*operands)


def copy_all(pairs, sems):
    copies = [pltpu.make_async_copy(src, dst, sems.at[n]) for n, (src, dst) in enumerate(pairs)]
    for copy in copies:
        copy.start()
    return copies


def units_of(place, shift, share):
    start = lax.rem(place[CHIP] + shift, CHIPS) * share
    return pl.ds(pl.multiple_of(start, 16), share)


def first_body(place, routes_hbm, tokens_hbm, w_gate, w_up, mine, *refs):
    *pieces, routes_t, sems = refs
    top, rows = routes_t.shape
    cols = mine.shape[1] // CHIPS
    share = pieces[0].shape[0] // 2
    pairs = [(routes_hbm, routes_t)]
    for shift in range(CHIPS):
        block = lax.rem(place[CHIP] - shift + CHIPS, CHIPS) * 2 + place[CORE]
        columns = pl.ds(pl.multiple_of(block * cols, cols), cols)
        pairs.append((tokens_hbm.at[:, columns], mine.at[:rows, shift * cols : (shift + 1) * cols]))
    for shift, out in enumerate(pieces, 1):
        pairs.append((w_gate.at[units_of(place, shift, share), :], out.at[:share, :]))
        pairs.append((w_up.at[units_of(place, shift, share), :], out.at[share:, :]))
    copies = copy_all(pairs, sems)
    mine[rows:, :] = jnp.zeros((mine.shape[0] - rows, mine.shape[1]), mine.dtype)
    copies[0].wait()
    mine[rows : rows + top, :rows] = routes_t[...].astype(mine.dtype)
    for copy in copies[1:]:
        copy.wait()


def hold_body(place, w_gate, w_up, one, three, _, here, one_out, three_out, sems):
    share = here.shape[0] // 2
    pairs = [
        (w.at[units_of(place, 0, share), :], here.at[n * share : (n + 1) * share, :])
        for n, w in enumerate((w_gate, w_up))
    ]
    copies = copy_all(pairs, sems)
    one_out[...] = one[...]
    three_out[...] = three[...]
    for copy in copies:
        copy.wait()


def picked(top, cap, experts, side, place, block, target_t=None):
    rows = block.shape[0] - 16
    slots = side * cap
    routes_t = block[rows:, :rows].astype(jnp.float32).astype(jnp.int32)
    expert_ids = lax.broadcasted_iota(jnp.int32, (experts, rows), 0)
    chosen = [(routes_t[k : k + 1, :] == expert_ids).astype(jnp.float32) for k in range(top)]
    named = functools.reduce(jnp.add, chosen)
    earlier = (
        lax.broadcasted_iota(jnp.int32, (rows, rows), 0) < lax.broadcasted_iota(jnp.int32, (rows, rows), 1)
    ).astype(jnp.bfloat16)
    before = jnp.dot(named.astype(jnp.bfloat16), earlier, preferred_element_type=jnp.float32)
    slot_ids = lax.broadcasted_iota(jnp.int32, (slots, rows), 0)
    picker = jnp.zeros((slots, rows), jnp.float32)
    for k in range(top):
        slot = jnp.sum(chosen[k] * before, axis=0, keepdims=True).astype(jnp.int32)
        target = routes_t[k : k + 1, :] * cap + slot
        if target_t is not None:
            target_t[k : k + 1, :] = target
        picker += (slot_ids == target - place[SIDE] * slots).astype(jnp.float32)
    rows_out = jnp.dot(picker.astype(jnp.bfloat16), block[:rows, :], preferred_element_type=jnp.float32)
    return rows_out.astype(jnp.bfloat16).reshape(side, cap, block.shape[1] // 128, 128)


def own_body(sizes, place, mine, out, target_t):
    out[...] = picked(*sizes, place, mine, target_t)


def dispatch_body(sizes, place, own, neighbour, outgoing):
    outgoing[:, 1 - place[SIDE]] = picked(*sizes, place, neighbour)
    outgoing[:, place[SIDE]] = own[...]


def gate_up_body(mine, place, rows, *refs):
    *weights, out = refs
    half, cols = out.shape[0], weights[0].shape[1]
    for core in range(2):
        start = (core if mine else 1 - core) * (rows.shape[0] // 2)

        @pl.when(place[CORE] == core)
        def _():
            flat = rows[start : start + rows.shape[0] // 2].reshape(half, CHIPS * cols)
            total = functools.reduce(
                jnp.add,
                [
                    lax.dot_general(
                        flat[:, n * cols : (n + 1) * cols], w[...], NT, preferred_element_type=jnp.float32
                    )
                    for n, w in enumerate(weights)
                ],
            )
            out[...] = total.astype(out.dtype)


def hidden_body(mine, theirs, hidden):
    total = mine[...] + theirs[...].astype(jnp.float32)
    half, units = total.shape[0], total.shape[1] // 2
    gate, up = total[:, :units], total[:, units:]
    value = gate / (1 + jnp.exp(-gate)) * up
    full = units // 128
    rows = half // GROUPS
    for n in range(full):
        hidden[n * half : (n + 1) * half, :] = value[:, n * 128 : (n + 1) * 128].astype(jnp.bfloat16)
    rest = jnp.concatenate([value[g * rows : (g + 1) * rows, full * 128 :] for g in range(GROUPS)], 1)
    for n in range(rest.shape[1] // 128):
        start = full * half + n * rows
        hidden[start : start + rows, :] = rest[:, n * 128 : (n + 1) * 128].astype(jnp.bfloat16)


def down(hidden, w_down):
    units = w_down.shape[0] // CHIPS
    full, left = units // 128, units % 128
    half = hidden.shape[1] * 128 // units
    rows = half // GROUPS
    total = jnp.zeros((half, w_down.shape[1]), jnp.float32)
    for z in range(CHIPS):
        main = jnp.concatenate([hidden[z, n * half : (n + 1) * half, :] for n in range(full)], 1)
        rest = [
            hidden[z, full * half + n * rows : full * half + (n + 1) * rows, :].astype(jnp.float32)
            for n in range(GROUPS * left // 128)
        ]
        rest = jnp.concatenate(rest, 1)
        rest = jnp.concatenate([rest[:, g * left : (g + 1) * left] for g in range(GROUPS)], 0)
        start = z * units
        total += jnp.dot(main, w_down[start : start + full * 128, :], preferred_element_type=jnp.float32)
        total += jnp.dot(
            rest.astype(jnp.bfloat16),
            w_down[start + full * 128 : start + units, :],
            preferred_element_type=jnp.float32,
        )
    return total.astype(jnp.bfloat16)


def down_own_body(own, w_down, out):
    out[...] = down(own, w_down)


def down_body(place, own, other, w_down, out):
    blocks, cap = out.shape[:2]
    part = blocks // 4
    for value, which in ((own[...], place[CORE]), (down(other, w_down), 1 - place[CORE])):
        value = value.reshape(part, 2, cap, *out.shape[2:])
        for side in range(2):
            out[pl.ds(side * (blocks // 2) + which * part, part)] = value[:, side]


def combine_body(target_t, weight_t, returned, out):
    top, rows = target_t.shape
    slots = returned.shape[0] * returned.shape[1]
    slot_ids = lax.broadcasted_iota(jnp.int32, (slots, rows), 0)
    spread = jnp.zeros((slots, rows), jnp.float32)
    for k in range(top):
        spread += jnp.where(slot_ids == target_t[k : k + 1, :], weight_t[k : k + 1, :], 0.0)
    high = spread.astype(jnp.bfloat16)
    low = (spread - high.astype(jnp.float32)).astype(jnp.bfloat16)
    flat = returned[...].reshape(slots, out.shape[1])
    total = lax.dot_general(high, flat, TN, preferred_element_type=jnp.float32)
    total += lax.dot_general(low, flat, TN, preferred_element_type=jnp.float32)
    out[...] = total.astype(jnp.bfloat16)


def on_device(tokens, routes, route_weight, w_gate, w_up, w_down):
    tok_count, top = routes.shape
    _, units, cols = w_gate.shape
    side = lax.axis_size("plane")
    experts = 2 * side
    cap = max(2, (11 * tok_count + experts - 1) // experts)
    slots = experts * cap
    share = units // CHIPS
    half = slots // 2
    bf16 = jnp.bfloat16
    dma = pltpu.SemaphoreType.DMA
    swap = [(0, 1), (1, 0)]
    place = jnp.stack([lax.axis_index(a) for a in ("core", "chip", "side")]).astype(jnp.int32)

    part = jax.ShapeDtypeStruct((2 * share, cols), bf16)
    mine, one, two, three = call(
        first_body,
        (jax.ShapeDtypeStruct((tok_count + 16, CHIPS * cols), bf16),) + (part,) * (CHIPS - 1),
        place,
        routes.T,
        tokens,
        w_gate[0],
        w_up[0],
        scalars=1,
        raw=4,
        scratch=[pltpu.VMEM((top, tok_count), jnp.int32), dma((3 * CHIPS - 1,))],
    )
    neighbour = lax.ppermute(mine, "side", swap)
    sizes = (top, cap, experts, side)
    chunk = (cap, CHIPS * cols // 128, 128)
    picked_own, target_t = call(
        functools.partial(own_body, sizes),
        (
            jax.ShapeDtypeStruct((side, *chunk), bf16),
            jax.ShapeDtypeStruct((top, tok_count), jnp.int32),
        ),
        place,
        mine,
        scalars=1,
    )
    outgoing = call(
        functools.partial(dispatch_body, sizes),
        jax.ShapeDtypeStruct((side, 2, *chunk), bf16),
        place,
        picked_own,
        neighbour,
        scalars=1,
        flops=PICK,
    )
    received = lax.all_to_all(outgoing, "plane", split_axis=0, concat_axis=0, tiled=True)
    ring = [[(i, (i + shift) % CHIPS) for i in range(CHIPS)] for shift in range(CHIPS)]
    two = lax.ppermute(two, "chip", ring[2])
    here, one, three = call(
        hold_body,
        (part,) * 3,
        place,
        w_gate[0],
        w_up[0],
        one,
        three,
        two,
        scalars=1,
        raw=2,
        scratch=[dma((2,))],
        flops=HOLD,
    )
    one = lax.ppermute(one, "chip", ring[1])
    three = lax.ppermute(three, "chip", ring[3])
    weights = (here, one, two, three)
    theirs = call(
        functools.partial(gate_up_body, False),
        jax.ShapeDtypeStruct((half, 2 * share), bf16),
        place,
        received,
        *weights,
        scalars=1,
    )
    theirs = lax.ppermute(theirs, "core", swap)
    mine = call(
        functools.partial(gate_up_body, True),
        jax.ShapeDtypeStruct((half, 2 * share), jnp.float32),
        place,
        received,
        *weights,
        scalars=1,
    )
    hidden = call(hidden_body, jax.ShapeDtypeStruct((half * share // 128, 128), bf16), mine, theirs)
    own = lax.all_gather(hidden, "chip", axis=0)
    other = lax.ppermute(own, "core", swap)
    produced = call(
        down_body,
        jax.ShapeDtypeStruct((experts, cap, cols // 128, 128), bf16),
        place,
        call(down_own_body, jax.ShapeDtypeStruct((half, cols), bf16), own, w_down[0]),
        other,
        w_down[0],
        scalars=1,
    )
    returned = lax.all_to_all(produced, ("side", "plane"), split_axis=0, concat_axis=0, tiled=True)
    return call(
        combine_body,
        jax.ShapeDtypeStruct((tok_count, cols), bf16),
        target_t,
        route_weight.T,
        returned,
    )


def solution(mesh):
    fine = Mesh(
        mesh.devices.reshape(2, mesh.shape["wide"] // 2, CHIPS, 2), ("side", "plane", "chip", "core")
    )
    wide, narrow = ("side", "plane"), ("chip", "core")
    return jax.shard_map(
        on_device,
        mesh=fine,
        in_specs=(
            P(wide, None),
            P(wide, None),
            P(wide, None),
            P(wide, None, narrow),
            P(wide, None, narrow),
            P(wide, None, narrow),
        ),
        out_specs=P(wide, narrow),
        check_vma=False,
    )
```

```python
import functools

import jax
import jax.numpy as jnp
from jax import lax
from jax.experimental import pallas as pl
from jax.experimental.pallas import tpu as pltpu
from jax.sharding import Mesh
from jax.sharding import PartitionSpec as P

VMEM = pl.BlockSpec(memory_space=pltpu.VMEM)
HBM = pl.BlockSpec(memory_space=pltpu.HBM)
SMEM = pl.BlockSpec(memory_space=pltpu.SMEM)
NT = (((1,), (1,)), ((), ()))
TN = (((0,), (0,)), ((), ()))


HOLD = 30_000_000_000
PICK = 10_000_000_000
CHIPS = 4
GROUPS = 4
CORE, CHIP, SIDE = range(3)


def call(body, outs, *operands, scalars=0, raw=0, scratch=(), flops=None, out_space=VMEM):
    operands = list(operands)
    for n in range(scalars, scalars + raw):
        operands[n] = pltpu.with_memory_space_constraint(operands[n], pltpu.HBM)
    cost = None if flops is None else pl.CostEstimate(flops=flops, transcendentals=0, bytes_accessed=0)
    return pl.pallas_call(
        body,
        out_shape=outs,
        in_specs=[SMEM] * scalars + [HBM] * raw + [VMEM] * (len(operands) - scalars - raw),
        out_specs=jax.tree.map(lambda _: out_space, outs),
        scratch_shapes=scratch,
        cost_estimate=cost,
        compiler_params=pltpu.CompilerParams(vmem_limit_bytes=16 << 20),
    )(*operands)


def copy_all(pairs, sems):
    copies = [pltpu.make_async_copy(src, dst, sems.at[n]) for n, (src, dst) in enumerate(pairs)]
    for copy in copies:
        copy.start()
    return copies


def units_of(place, shift, share):
    start = lax.rem(place[CHIP] + shift, CHIPS) * share
    return pl.ds(pl.multiple_of(start, 16), share)


def slices(place, w_gate, w_up, shift, out):
    share = out.shape[0] // 2
    return [
        (w.at[units_of(place, shift, share), :], out.at[n * share : (n + 1) * share, :])
        for n, w in enumerate((w_gate, w_up))
    ]


def first_body(place, routes_hbm, tokens_hbm, w_gate, w_up, mine, *refs):
    two, routes_t, sems = refs
    top, rows = routes_t.shape
    cols = mine.shape[1] // CHIPS
    pairs = [(routes_hbm, routes_t)]
    for shift in range(CHIPS):
        block = lax.rem(place[CHIP] - shift + CHIPS, CHIPS) * 2 + place[CORE]
        columns = pl.ds(pl.multiple_of(block * cols, cols), cols)
        pairs.append((tokens_hbm.at[:, columns], mine.at[:rows, shift * cols : (shift + 1) * cols]))
    pairs += slices(place, w_gate, w_up, 2, two)
    copies = copy_all(pairs, sems)
    mine[rows:, :] = jnp.zeros((mine.shape[0] - rows, mine.shape[1]), mine.dtype)
    copies[0].wait()
    mine[rows : rows + top, :rows] = routes_t[...].astype(mine.dtype)
    for copy in copies[1:]:
        copy.wait()


def hold_body(place, w_gate, w_up, one, three, _, here, one_out, three_out, sems):
    copies = copy_all(slices(place, w_gate, w_up, 0, here), sems)
    one_out[...] = one[...]
    three_out[...] = three[...]
    for copy in copies:
        copy.wait()


def picked(top, cap, experts, side, place, block, target_t=None):
    rows = block.shape[0] - 16
    slots = side * cap
    routes_t = block[rows:, :rows].astype(jnp.float32).astype(jnp.int32)
    expert_ids = lax.broadcasted_iota(jnp.int32, (experts, rows), 0)
    chosen = [(routes_t[k : k + 1, :] == expert_ids).astype(jnp.float32) for k in range(top)]
    named = functools.reduce(jnp.add, chosen)
    earlier = (
        lax.broadcasted_iota(jnp.int32, (rows, rows), 0) < lax.broadcasted_iota(jnp.int32, (rows, rows), 1)
    ).astype(jnp.bfloat16)
    before = jnp.dot(named.astype(jnp.bfloat16), earlier, preferred_element_type=jnp.float32)
    slot_ids = lax.broadcasted_iota(jnp.int32, (slots, rows), 0)
    picker = jnp.zeros((slots, rows), jnp.float32)
    for k in range(top):
        slot = jnp.sum(chosen[k] * before, axis=0, keepdims=True).astype(jnp.int32)
        target = routes_t[k : k + 1, :] * cap + slot
        if target_t is not None:
            target_t[k : k + 1, :] = target
        picker += (slot_ids == target - place[SIDE] * slots).astype(jnp.float32)
    rows_out = jnp.dot(picker.astype(jnp.bfloat16), block[:rows, :], preferred_element_type=jnp.float32)
    return rows_out.astype(jnp.bfloat16).reshape(side, cap, block.shape[1] // 128, 128)


def dispatch_body(sizes, place, w_gate, w_up, mine, neighbour, outgoing, target_t, one, three, sems):
    pairs = slices(place, w_gate, w_up, 1, one) + slices(place, w_gate, w_up, 3, three)
    copies = copy_all(pairs, sems)
    outgoing[:, place[SIDE]] = picked(*sizes, place, mine, target_t)
    outgoing[:, 1 - place[SIDE]] = picked(*sizes, place, neighbour)
    for copy in copies:
        copy.wait()


def gate_up_body(mine, place, rows, *refs):
    *weights, out = refs
    half, cols = out.shape[0], weights[0].shape[1]
    for core in range(2):
        start = (core if mine else 1 - core) * (rows.shape[0] // 2)

        @pl.when(place[CORE] == core)
        def _():
            flat = rows[start : start + rows.shape[0] // 2].reshape(half, CHIPS * cols)
            total = functools.reduce(
                jnp.add,
                [
                    lax.dot_general(
                        flat[:, n * cols : (n + 1) * cols], w[...], NT, preferred_element_type=jnp.float32
                    )
                    for n, w in enumerate(weights)
                ],
            )
            out[...] = total.astype(out.dtype)


def hidden_body(mine, theirs, hidden):
    total = mine[...] + theirs[...].astype(jnp.float32)
    half, units = total.shape[0], total.shape[1] // 2
    gate, up = total[:, :units], total[:, units:]
    value = gate / (1 + jnp.exp(-gate)) * up
    full = units // 128
    rows = half // GROUPS
    for n in range(full):
        hidden[n * half : (n + 1) * half, :] = value[:, n * 128 : (n + 1) * 128].astype(jnp.bfloat16)
    rest = jnp.concatenate([value[g * rows : (g + 1) * rows, full * 128 :] for g in range(GROUPS)], 1)
    for n in range(rest.shape[1] // 128):
        start = full * half + n * rows
        hidden[start : start + rows, :] = rest[:, n * 128 : (n + 1) * 128].astype(jnp.bfloat16)


def down(hidden, w_down):
    units = w_down.shape[0] // CHIPS
    full, left = units // 128, units % 128
    half = hidden.shape[1] * 128 // units
    rows = half // GROUPS
    total = jnp.zeros((half, w_down.shape[1]), jnp.float32)
    for z in range(CHIPS):
        main = jnp.concatenate([hidden[z, n * half : (n + 1) * half, :] for n in range(full)], 1)
        rest = [
            hidden[z, full * half + n * rows : full * half + (n + 1) * rows, :].astype(jnp.float32)
            for n in range(GROUPS * left // 128)
        ]
        rest = jnp.concatenate(rest, 1)
        rest = jnp.concatenate([rest[:, g * left : (g + 1) * left] for g in range(GROUPS)], 0)
        start = z * units
        total += jnp.dot(main, w_down[start : start + full * 128, :], preferred_element_type=jnp.float32)
        total += jnp.dot(
            rest.astype(jnp.bfloat16),
            w_down[start + full * 128 : start + units, :],
            preferred_element_type=jnp.float32,
        )
    return total.astype(jnp.bfloat16)


def down_own_body(own, w_down, out):
    out[...] = down(own, w_down)


def down_body(place, own, other, w_down, out):
    blocks, cap = out.shape[:2]
    part = blocks // 4
    for value, which in ((own[...], place[CORE]), (down(other, w_down), 1 - place[CORE])):
        value = value.reshape(part, 2, cap, *out.shape[2:])
        for side in range(2):
            out[pl.ds(side * (blocks // 2) + which * part, part)] = value[:, side]


def combine_body(target_t, weight_t, returned, out):
    top, rows = target_t.shape
    slots = returned.shape[0] * returned.shape[1]
    slot_ids = lax.broadcasted_iota(jnp.int32, (slots, rows), 0)
    spread = jnp.zeros((slots, rows), jnp.float32)
    for k in range(top):
        spread += jnp.where(slot_ids == target_t[k : k + 1, :], weight_t[k : k + 1, :], 0.0)
    high = spread.astype(jnp.bfloat16)
    low = (spread - high.astype(jnp.float32)).astype(jnp.bfloat16)
    flat = returned[...].reshape(slots, out.shape[1])
    total = lax.dot_general(high, flat, TN, preferred_element_type=jnp.float32)
    total += lax.dot_general(low, flat, TN, preferred_element_type=jnp.float32)
    out[...] = total.astype(jnp.bfloat16)


def on_device(tokens, routes, route_weight, w_gate, w_up, w_down):
    tok_count, top = routes.shape
    _, units, cols = w_gate.shape
    side = lax.axis_size("plane")
    experts = 2 * side
    cap = max(2, (11 * tok_count + experts - 1) // experts)
    slots = experts * cap
    share = units // CHIPS
    half = slots // 2
    bf16 = jnp.bfloat16
    dma = pltpu.SemaphoreType.DMA
    swap = [(0, 1), (1, 0)]
    place = jnp.stack([lax.axis_index(a) for a in ("core", "chip", "side")]).astype(jnp.int32)

    part = jax.ShapeDtypeStruct((2 * share, cols), bf16)
    mine, two = call(
        first_body,
        (jax.ShapeDtypeStruct((tok_count + 16, CHIPS * cols), bf16),) + (part,),
        place,
        routes.T,
        tokens,
        w_gate[0],
        w_up[0],
        scalars=1,
        raw=4,
        scratch=[pltpu.VMEM((top, tok_count), jnp.int32), dma((CHIPS + 3,))],
    )
    neighbour = lax.ppermute(mine, "side", swap)
    sizes = (top, cap, experts, side)
    chunk = (cap, CHIPS * cols // 128, 128)
    outgoing, target_t, one, three = call(
        functools.partial(dispatch_body, sizes),
        (
            jax.ShapeDtypeStruct((side, 2, *chunk), bf16),
            jax.ShapeDtypeStruct((top, tok_count), jnp.int32),
            part,
            part,
        ),
        place,
        w_gate[0],
        w_up[0],
        mine,
        neighbour,
        scalars=1,
        raw=2,
        scratch=[dma((4,))],
        flops=PICK,
    )
    received = lax.all_to_all(outgoing, "plane", split_axis=0, concat_axis=0, tiled=True)
    ring = [[(i, (i + shift) % CHIPS) for i in range(CHIPS)] for shift in range(CHIPS)]
    two = lax.ppermute(two, "chip", ring[2])
    here, one, three = call(
        hold_body,
        (part,) * 3,
        place,
        w_gate[0],
        w_up[0],
        one,
        three,
        two,
        scalars=1,
        raw=2,
        scratch=[dma((2,))],
        flops=HOLD,
    )
    one = lax.ppermute(one, "chip", ring[1])
    three = lax.ppermute(three, "chip", ring[3])
    weights = (here, one, two, three)
    theirs = call(
        functools.partial(gate_up_body, False),
        jax.ShapeDtypeStruct((half, 2 * share), bf16),
        place,
        received,
        *weights,
        scalars=1,
    )
    theirs = lax.ppermute(theirs, "core", swap)
    mine = call(
        functools.partial(gate_up_body, True),
        jax.ShapeDtypeStruct((half, 2 * share), jnp.float32),
        place,
        received,
        *weights,
        scalars=1,
    )
    hidden = call(hidden_body, jax.ShapeDtypeStruct((half * share // 128, 128), bf16), mine, theirs)
    own = lax.all_gather(hidden, "chip", axis=0)
    other = lax.ppermute(own, "core", swap)
    produced = call(
        down_body,
        jax.ShapeDtypeStruct((experts, cap, cols // 128, 128), bf16),
        place,
        call(down_own_body, jax.ShapeDtypeStruct((half, cols), bf16), own, w_down[0]),
        other,
        w_down[0],
        scalars=1,
    )
    returned = lax.all_to_all(produced, ("side", "plane"), split_axis=0, concat_axis=0, tiled=True)
    return call(
        combine_body,
        jax.ShapeDtypeStruct((tok_count, cols), bf16),
        target_t,
        route_weight.T,
        returned,
    )


def solution(mesh):
    fine = Mesh(
        mesh.devices.reshape(2, mesh.shape["wide"] // 2, CHIPS, 2), ("side", "plane", "chip", "core")
    )
    wide, narrow = ("side", "plane"), ("chip", "core")
    return jax.shard_map(
        on_device,
        mesh=fine,
        in_specs=(
            P(wide, None),
            P(wide, None),
            P(wide, None),
            P(wide, None, narrow),
            P(wide, None, narrow),
            P(wide, None, narrow),
        ),
        out_specs=P(wide, narrow),
        check_vma=False,
    )
```

```python
import functools

import jax
import jax.numpy as jnp
from jax import lax
from jax.experimental import pallas as pl
from jax.experimental.pallas import tpu as pltpu
from jax.sharding import Mesh
from jax.sharding import PartitionSpec as P

VMEM = pl.BlockSpec(memory_space=pltpu.VMEM)
HBM = pl.BlockSpec(memory_space=pltpu.HBM)
SMEM = pl.BlockSpec(memory_space=pltpu.SMEM)
NT = (((1,), (1,)), ((), ()))
TN = (((0,), (0,)), ((), ()))


HOLD = 30_000_000_000
PICK = 10_000_000_000
CHIPS = 4
GROUPS = 4
CORE, CHIP = range(2)


def call(body, outs, *operands, scalars=0, raw=0, scratch=(), flops=None, out_space=VMEM):
    operands = list(operands)
    for n in range(scalars, scalars + raw):
        operands[n] = pltpu.with_memory_space_constraint(operands[n], pltpu.HBM)
    cost = None if flops is None else pl.CostEstimate(flops=flops, transcendentals=0, bytes_accessed=0)
    return pl.pallas_call(
        body,
        out_shape=outs,
        in_specs=[SMEM] * scalars + [HBM] * raw + [VMEM] * (len(operands) - scalars - raw),
        out_specs=jax.tree.map(lambda _: out_space, outs),
        scratch_shapes=scratch,
        cost_estimate=cost,
        compiler_params=pltpu.CompilerParams(vmem_limit_bytes=16 << 20),
    )(*operands)


def copy_all(pairs, sems):
    copies = [pltpu.make_async_copy(src, dst, sems.at[n]) for n, (src, dst) in enumerate(pairs)]
    for copy in copies:
        copy.start()
    return copies


def units_of(place, shift, share):
    start = lax.rem(place[CHIP] + shift, CHIPS) * share
    return pl.ds(pl.multiple_of(start, 16), share)


def slices(place, w_gate, w_up, shift, out):
    share = out.shape[0] // 2
    return [
        (w.at[units_of(place, shift, share), :], out.at[n * share : (n + 1) * share, :])
        for n, w in enumerate((w_gate, w_up))
    ]


def first_body(place, routes_hbm, tokens_hbm, w_gate, w_up, mine, *refs):
    two, routes_t, sems = refs
    top, rows = routes_t.shape
    cols = mine.shape[1] // CHIPS
    pairs = [(routes_hbm, routes_t)]
    for shift in range(CHIPS):
        block = lax.rem(place[CHIP] - shift + CHIPS, CHIPS) * 2 + place[CORE]
        columns = pl.ds(pl.multiple_of(block * cols, cols), cols)
        pairs.append((tokens_hbm.at[:, columns], mine.at[:rows, shift * cols : (shift + 1) * cols]))
    pairs += slices(place, w_gate, w_up, 2, two)
    copies = copy_all(pairs, sems)
    mine[rows:, :] = jnp.zeros((mine.shape[0] - rows, mine.shape[1]), mine.dtype)
    copies[0].wait()
    mine[rows : rows + top, :rows] = routes_t[...].astype(mine.dtype)
    for copy in copies[1:]:
        copy.wait()


def hold_body(place, w_gate, w_up, one, three, _, here, one_out, three_out, sems):
    copies = copy_all(slices(place, w_gate, w_up, 0, here), sems)
    one_out[...] = one[...]
    three_out[...] = three[...]
    for copy in copies:
        copy.wait()


def picked(top, cap, experts, block, target_t):
    rows = block.shape[0] - 16
    slots = experts * cap
    routes_t = block[rows:, :rows].astype(jnp.float32).astype(jnp.int32)
    expert_ids = lax.broadcasted_iota(jnp.int32, (experts, rows), 0)
    chosen = [(routes_t[k : k + 1, :] == expert_ids).astype(jnp.float32) for k in range(top)]
    named = functools.reduce(jnp.add, chosen)
    earlier = (
        lax.broadcasted_iota(jnp.int32, (rows, rows), 0) < lax.broadcasted_iota(jnp.int32, (rows, rows), 1)
    ).astype(jnp.bfloat16)
    before = jnp.dot(named.astype(jnp.bfloat16), earlier, preferred_element_type=jnp.float32)
    slot_ids = lax.broadcasted_iota(jnp.int32, (slots, rows), 0)
    picker = jnp.zeros((slots, rows), jnp.float32)
    for k in range(top):
        slot = jnp.sum(chosen[k] * before, axis=0, keepdims=True).astype(jnp.int32)
        target = routes_t[k : k + 1, :] * cap + slot
        target_t[k : k + 1, :] = target
        picker += (slot_ids == target).astype(jnp.float32)
    rows_out = jnp.dot(picker.astype(jnp.bfloat16), block[:rows, :], preferred_element_type=jnp.float32)
    return rows_out.astype(jnp.bfloat16).reshape(experts, cap, block.shape[1] // 128, 128)


def dispatch_body(sizes, place, w_gate, w_up, mine, outgoing, target_t, one, three, sems):
    pairs = slices(place, w_gate, w_up, 1, one) + slices(place, w_gate, w_up, 3, three)
    copies = copy_all(pairs, sems)
    outgoing[...] = picked(*sizes, mine, target_t)
    for copy in copies:
        copy.wait()


def gate_up_body(mine, place, rows, *refs):
    *weights, out = refs
    half, cols = out.shape[0], weights[0].shape[1]
    for core in range(2):
        start = (core if mine else 1 - core) * (rows.shape[0] // 2)

        @pl.when(place[CORE] == core)
        def _():
            flat = rows[start : start + rows.shape[0] // 2].reshape(half, CHIPS * cols)
            total = functools.reduce(
                jnp.add,
                [
                    lax.dot_general(
                        flat[:, n * cols : (n + 1) * cols], w[...], NT, preferred_element_type=jnp.float32
                    )
                    for n, w in enumerate(weights)
                ],
            )
            out[...] = total.astype(out.dtype)


def hidden_body(mine, theirs, hidden):
    total = mine[...] + theirs[...].astype(jnp.float32)
    half, units = total.shape[0], total.shape[1] // 2
    gate, up = total[:, :units], total[:, units:]
    value = gate / (1 + jnp.exp(-gate)) * up
    full = units // 128
    rows = half // GROUPS
    for n in range(full):
        hidden[n * half : (n + 1) * half, :] = value[:, n * 128 : (n + 1) * 128].astype(jnp.bfloat16)
    rest = jnp.concatenate([value[g * rows : (g + 1) * rows, full * 128 :] for g in range(GROUPS)], 1)
    for n in range(rest.shape[1] // 128):
        start = full * half + n * rows
        hidden[start : start + rows, :] = rest[:, n * 128 : (n + 1) * 128].astype(jnp.bfloat16)


def down(hidden, w_down):
    units = w_down.shape[0] // CHIPS
    full, left = units // 128, units % 128
    half = hidden.shape[1] * 128 // units
    rows = half // GROUPS
    total = jnp.zeros((half, w_down.shape[1]), jnp.float32)
    for z in range(CHIPS):
        main = jnp.concatenate([hidden[z, n * half : (n + 1) * half, :] for n in range(full)], 1)
        rest = [
            hidden[z, full * half + n * rows : full * half + (n + 1) * rows, :].astype(jnp.float32)
            for n in range(GROUPS * left // 128)
        ]
        rest = jnp.concatenate(rest, 1)
        rest = jnp.concatenate([rest[:, g * left : (g + 1) * left] for g in range(GROUPS)], 0)
        start = z * units
        total += jnp.dot(main, w_down[start : start + full * 128, :], preferred_element_type=jnp.float32)
        total += jnp.dot(
            rest.astype(jnp.bfloat16),
            w_down[start + full * 128 : start + units, :],
            preferred_element_type=jnp.float32,
        )
    return total.astype(jnp.bfloat16)


def down_own_body(own, w_down, out):
    out[...] = down(own, w_down)


def down_body(place, own, other, w_down, out):
    cap = out.shape[1]
    part = out.shape[0] // 2
    for value, which in ((own[...], place[CORE]), (down(other, w_down), 1 - place[CORE])):
        out[pl.ds(which * part, part)] = value.reshape(part, cap, *out.shape[2:])


def combine_body(target_t, weight_t, returned, out):
    top, rows = target_t.shape
    slots = returned.shape[0] * returned.shape[1]
    slot_ids = lax.broadcasted_iota(jnp.int32, (slots, rows), 0)
    spread = jnp.zeros((slots, rows), jnp.float32)
    for k in range(top):
        spread += jnp.where(slot_ids == target_t[k : k + 1, :], weight_t[k : k + 1, :], 0.0)
    high = spread.astype(jnp.bfloat16)
    low = (spread - high.astype(jnp.float32)).astype(jnp.bfloat16)
    flat = returned[...].reshape(slots, out.shape[1])
    total = lax.dot_general(high, flat, TN, preferred_element_type=jnp.float32)
    total += lax.dot_general(low, flat, TN, preferred_element_type=jnp.float32)
    out[...] = total.astype(jnp.bfloat16)


def on_device(tokens, routes, route_weight, w_gate, w_up, w_down):
    tok_count, top = routes.shape
    _, units, cols = w_gate.shape
    experts = lax.axis_size("wide")
    cap = max(2, (11 * tok_count + experts - 1) // experts)
    slots = experts * cap
    share = units // CHIPS
    half = slots // 2
    bf16 = jnp.bfloat16
    dma = pltpu.SemaphoreType.DMA
    swap = [(0, 1), (1, 0)]
    place = jnp.stack([lax.axis_index(a) for a in ("core", "chip")]).astype(jnp.int32)

    part = jax.ShapeDtypeStruct((2 * share, cols), bf16)
    mine, two = call(
        first_body,
        (jax.ShapeDtypeStruct((tok_count + 16, CHIPS * cols), bf16),) + (part,),
        place,
        routes.T,
        tokens,
        w_gate[0],
        w_up[0],
        scalars=1,
        raw=4,
        scratch=[pltpu.VMEM((top, tok_count), jnp.int32), dma((CHIPS + 3,))],
    )
    sizes = (top, cap, experts)
    chunk = (cap, CHIPS * cols // 128, 128)
    outgoing, target_t, one, three = call(
        functools.partial(dispatch_body, sizes),
        (
            jax.ShapeDtypeStruct((experts, *chunk), bf16),
            jax.ShapeDtypeStruct((top, tok_count), jnp.int32),
            part,
            part,
        ),
        place,
        w_gate[0],
        w_up[0],
        mine,
        scalars=1,
        raw=2,
        scratch=[dma((4,))],
        flops=PICK,
    )
    received = lax.all_to_all(outgoing, "wide", split_axis=0, concat_axis=0, tiled=True)
    ring = [[(i, (i + shift) % CHIPS) for i in range(CHIPS)] for shift in range(CHIPS)]
    two = lax.ppermute(two, "chip", ring[2])
    here, one, three = call(
        hold_body,
        (part,) * 3,
        place,
        w_gate[0],
        w_up[0],
        one,
        three,
        two,
        scalars=1,
        raw=2,
        scratch=[dma((2,))],
        flops=HOLD,
    )
    one = lax.ppermute(one, "chip", ring[1])
    three = lax.ppermute(three, "chip", ring[3])
    weights = (here, one, two, three)
    theirs = call(
        functools.partial(gate_up_body, False),
        jax.ShapeDtypeStruct((half, 2 * share), bf16),
        place,
        received,
        *weights,
        scalars=1,
    )
    theirs = lax.ppermute(theirs, "core", swap)
    mine = call(
        functools.partial(gate_up_body, True),
        jax.ShapeDtypeStruct((half, 2 * share), jnp.float32),
        place,
        received,
        *weights,
        scalars=1,
    )
    hidden = call(hidden_body, jax.ShapeDtypeStruct((half * share // 128, 128), bf16), mine, theirs)
    own = lax.all_gather(hidden, "chip", axis=0)
    other = lax.ppermute(own, "core", swap)
    produced = call(
        down_body,
        jax.ShapeDtypeStruct((experts, cap, cols // 128, 128), bf16),
        place,
        call(down_own_body, jax.ShapeDtypeStruct((half, cols), bf16), own, w_down[0]),
        other,
        w_down[0],
        scalars=1,
    )
    returned = lax.all_to_all(produced, "wide", split_axis=0, concat_axis=0, tiled=True)
    return call(
        combine_body,
        jax.ShapeDtypeStruct((tok_count, cols), bf16),
        target_t,
        route_weight.T,
        returned,
    )


def solution(mesh):
    fine = Mesh(mesh.devices.reshape(mesh.shape["wide"], CHIPS, 2), ("wide", "chip", "core"))
    wide, narrow = "wide", ("chip", "core")
    return jax.shard_map(
        on_device,
        mesh=fine,
        in_specs=(
            P(wide, None),
            P(wide, None),
            P(wide, None),
            P(wide, None, narrow),
            P(wide, None, narrow),
            P(wide, None, narrow),
        ),
        out_specs=P(wide, narrow),
        check_vma=False,
    )
```

```python
import functools

import jax
import jax.numpy as jnp
from jax import lax
from jax.experimental import pallas as pl
from jax.experimental.pallas import tpu as pltpu
from jax.sharding import Mesh
from jax.sharding import PartitionSpec as P

VMEM = pl.BlockSpec(memory_space=pltpu.VMEM)
HBM = pl.BlockSpec(memory_space=pltpu.HBM)
SMEM = pl.BlockSpec(memory_space=pltpu.SMEM)
NT = (((1,), (1,)), ((), ()))
TN = (((0,), (0,)), ((), ()))


HOLD = 30_000_000_000
PICK = 10_000_000_000
CHIPS = 4
GROUPS = 4
CORE, CHIP, SIDE = range(3)


def call(body, outs, *operands, scalars=0, raw=0, scratch=(), flops=None, out_space=VMEM):
    operands = list(operands)
    for n in range(scalars, scalars + raw):
        operands[n] = pltpu.with_memory_space_constraint(operands[n], pltpu.HBM)
    cost = None if flops is None else pl.CostEstimate(flops=flops, transcendentals=0, bytes_accessed=0)
    return pl.pallas_call(
        body,
        out_shape=outs,
        in_specs=[SMEM] * scalars + [HBM] * raw + [VMEM] * (len(operands) - scalars - raw),
        out_specs=jax.tree.map(lambda _: out_space, outs),
        scratch_shapes=scratch,
        cost_estimate=cost,
        compiler_params=pltpu.CompilerParams(vmem_limit_bytes=16 << 20),
    )(*operands)


def copy_all(pairs, sems):
    copies = [pltpu.make_async_copy(src, dst, sems.at[n]) for n, (src, dst) in enumerate(pairs)]
    for copy in copies:
        copy.start()
    return copies


def units_of(place, shift, share):
    start = lax.rem(place[CHIP] + shift, CHIPS) * share
    return pl.ds(pl.multiple_of(start, 16), share)


def slices(place, w_gate, w_up, shift, out):
    share = out.shape[0] // 2
    return [
        (w.at[units_of(place, shift, share), :], out.at[n * share : (n + 1) * share, :])
        for n, w in enumerate((w_gate, w_up))
    ]


def first_body(place, routes_hbm, tokens_hbm, w_gate, w_up, mine, *refs):
    two, routes_t, sems = refs
    top, rows = routes_t.shape
    cols = mine.shape[1] // CHIPS
    pairs = [(routes_hbm, routes_t)]
    for shift in range(CHIPS):
        block = lax.rem(place[CHIP] - shift + CHIPS, CHIPS) * 2 + place[CORE]
        columns = pl.ds(pl.multiple_of(block * cols, cols), cols)
        pairs.append((tokens_hbm.at[:, columns], mine.at[:rows, shift * cols : (shift + 1) * cols]))
    pairs += slices(place, w_gate, w_up, 2, two)
    copies = copy_all(pairs, sems)
    mine[rows:, :] = jnp.zeros((mine.shape[0] - rows, mine.shape[1]), mine.dtype)
    copies[0].wait()
    mine[rows : rows + top, :rows] = routes_t[...].astype(mine.dtype)
    for copy in copies[1:]:
        copy.wait()


def hold_body(place, w_gate, w_up, one, three, _, here, one_out, three_out, sems):
    share = here.shape[0] // 2
    pairs = [
        (w.at[units_of(place, 0, share), :], here.at[n * share : (n + 1) * share, :])
        for n, w in enumerate((w_gate, w_up))
    ]
    copies = copy_all(pairs, sems)
    one_out[...] = one[...]
    three_out[...] = three[...]
    for copy in copies:
        copy.wait()


def picked(top, cap, experts, side, place, block, target_t=None):
    rows = block.shape[0] - 16
    slots = side * cap
    routes_t = block[rows:, :rows].astype(jnp.float32).astype(jnp.int32)
    expert_ids = lax.broadcasted_iota(jnp.int32, (experts, rows), 0)
    chosen = [(routes_t[k : k + 1, :] == expert_ids).astype(jnp.float32) for k in range(top)]
    named = functools.reduce(jnp.add, chosen)
    earlier = (
        lax.broadcasted_iota(jnp.int32, (rows, rows), 0) < lax.broadcasted_iota(jnp.int32, (rows, rows), 1)
    ).astype(jnp.bfloat16)
    before = jnp.dot(named.astype(jnp.bfloat16), earlier, preferred_element_type=jnp.float32)
    slot_ids = lax.broadcasted_iota(jnp.int32, (slots, rows), 0)
    picker = jnp.zeros((slots, rows), jnp.float32)
    for k in range(top):
        slot = jnp.sum(chosen[k] * before, axis=0, keepdims=True).astype(jnp.int32)
        target = routes_t[k : k + 1, :] * cap + slot
        if target_t is not None:
            target_t[k : k + 1, :] = target
        picker += (slot_ids == target - place[SIDE] * slots).astype(jnp.float32)
    rows_out = jnp.dot(picker.astype(jnp.bfloat16), block[:rows, :], preferred_element_type=jnp.float32)
    return rows_out.astype(jnp.bfloat16).reshape(side, cap, block.shape[1] // 128, 128)


def own_body(sizes, place, w_gate, w_up, mine, out, target_t, one, three, sems):
    pairs = slices(place, w_gate, w_up, 1, one) + slices(place, w_gate, w_up, 3, three)
    copies = copy_all(pairs, sems)
    out[...] = picked(*sizes, place, mine, target_t)
    for copy in copies:
        copy.wait()


def dispatch_body(sizes, place, own, neighbour, outgoing):
    outgoing[:, 1 - place[SIDE]] = picked(*sizes, place, neighbour)
    outgoing[:, place[SIDE]] = own[...]


def gate_up_body(mine, place, rows, *refs):
    *weights, out = refs
    half, cols = out.shape[0], weights[0].shape[1]
    for core in range(2):
        start = (core if mine else 1 - core) * (rows.shape[0] // 2)

        @pl.when(place[CORE] == core)
        def _():
            flat = rows[start : start + rows.shape[0] // 2].reshape(half, CHIPS * cols)
            total = functools.reduce(
                jnp.add,
                [
                    lax.dot_general(
                        flat[:, n * cols : (n + 1) * cols], w[...], NT, preferred_element_type=jnp.float32
                    )
                    for n, w in enumerate(weights)
                ],
            )
            out[...] = total.astype(out.dtype)


def hidden_body(mine, theirs, hidden):
    total = mine[...] + theirs[...].astype(jnp.float32)
    half, units = total.shape[0], total.shape[1] // 2
    gate, up = total[:, :units], total[:, units:]
    value = gate / (1 + jnp.exp(-gate)) * up
    full = units // 128
    rows = half // GROUPS
    for n in range(full):
        hidden[n * half : (n + 1) * half, :] = value[:, n * 128 : (n + 1) * 128].astype(jnp.bfloat16)
    rest = jnp.concatenate([value[g * rows : (g + 1) * rows, full * 128 :] for g in range(GROUPS)], 1)
    for n in range(rest.shape[1] // 128):
        start = full * half + n * rows
        hidden[start : start + rows, :] = rest[:, n * 128 : (n + 1) * 128].astype(jnp.bfloat16)


def down(hidden, w_down):
    units = w_down.shape[0] // CHIPS
    full, left = units // 128, units % 128
    half = hidden.shape[1] * 128 // units
    rows = half // GROUPS
    total = jnp.zeros((half, w_down.shape[1]), jnp.float32)
    for z in range(CHIPS):
        main = jnp.concatenate([hidden[z, n * half : (n + 1) * half, :] for n in range(full)], 1)
        rest = [
            hidden[z, full * half + n * rows : full * half + (n + 1) * rows, :].astype(jnp.float32)
            for n in range(GROUPS * left // 128)
        ]
        rest = jnp.concatenate(rest, 1)
        rest = jnp.concatenate([rest[:, g * left : (g + 1) * left] for g in range(GROUPS)], 0)
        start = z * units
        total += jnp.dot(main, w_down[start : start + full * 128, :], preferred_element_type=jnp.float32)
        total += jnp.dot(
            rest.astype(jnp.bfloat16),
            w_down[start + full * 128 : start + units, :],
            preferred_element_type=jnp.float32,
        )
    return total.astype(jnp.bfloat16)


def down_own_body(own, w_down, target_t, weight_t, out, high, low):
    out[...] = down(own, w_down)
    top = target_t.shape[0]
    slot_ids = lax.broadcasted_iota(jnp.int32, high.shape, 0)
    spread = jnp.zeros(high.shape, jnp.float32)
    for k in range(top):
        spread += jnp.where(slot_ids == target_t[k : k + 1, :], weight_t[k : k + 1, :], 0.0)
    high[...] = spread.astype(jnp.bfloat16)
    low[...] = (spread - high[...].astype(jnp.float32)).astype(jnp.bfloat16)


def down_body(place, own, other, w_down, out):
    blocks, cap = out.shape[:2]
    part = blocks // 4
    for value, which in ((own[...], place[CORE]), (down(other, w_down), 1 - place[CORE])):
        value = value.reshape(part, 2, cap, *out.shape[2:])
        for side in range(2):
            out[pl.ds(side * (blocks // 2) + which * part, part)] = value[:, side]


def combine_body(high, low, returned, out):
    flat = returned[...].reshape(high.shape[0], out.shape[1])
    total = lax.dot_general(high[...], flat, TN, preferred_element_type=jnp.float32)
    total += lax.dot_general(low[...], flat, TN, preferred_element_type=jnp.float32)
    out[...] = total.astype(jnp.bfloat16)


def on_device(tokens, routes, route_weight, w_gate, w_up, w_down):
    tok_count, top = routes.shape
    _, units, cols = w_gate.shape
    side = lax.axis_size("plane")
    experts = 2 * side
    cap = max(2, (11 * tok_count + experts - 1) // experts)
    slots = experts * cap
    share = units // CHIPS
    half = slots // 2
    bf16 = jnp.bfloat16
    dma = pltpu.SemaphoreType.DMA
    swap = [(0, 1), (1, 0)]
    place = jnp.stack([lax.axis_index(a) for a in ("core", "chip", "side")]).astype(jnp.int32)

    part = jax.ShapeDtypeStruct((2 * share, cols), bf16)
    mine, two = call(
        first_body,
        (jax.ShapeDtypeStruct((tok_count + 16, CHIPS * cols), bf16),) + (part,),
        place,
        routes.T,
        tokens,
        w_gate[0],
        w_up[0],
        scalars=1,
        raw=4,
        scratch=[pltpu.VMEM((top, tok_count), jnp.int32), dma((CHIPS + 3,))],
    )
    neighbour = lax.ppermute(mine, "side", swap)
    sizes = (top, cap, experts, side)
    chunk = (cap, CHIPS * cols // 128, 128)
    picked_own, target_t, one, three = call(
        functools.partial(own_body, sizes),
        (
            jax.ShapeDtypeStruct((side, *chunk), bf16),
            jax.ShapeDtypeStruct((top, tok_count), jnp.int32),
            part,
            part,
        ),
        place,
        w_gate[0],
        w_up[0],
        mine,
        scalars=1,
        raw=2,
        scratch=[dma((4,))],
    )
    outgoing = call(
        functools.partial(dispatch_body, sizes),
        jax.ShapeDtypeStruct((side, 2, *chunk), bf16),
        place,
        picked_own,
        neighbour,
        scalars=1,
        flops=PICK,
    )
    received = lax.all_to_all(outgoing, "plane", split_axis=0, concat_axis=0, tiled=True)
    ring = [[(i, (i + shift) % CHIPS) for i in range(CHIPS)] for shift in range(CHIPS)]
    two = lax.ppermute(two, "chip", ring[2])
    here, one, three = call(
        hold_body,
        (part,) * 3,
        place,
        w_gate[0],
        w_up[0],
        one,
        three,
        two,
        scalars=1,
        raw=2,
        scratch=[dma((2,))],
        flops=HOLD,
    )
    one = lax.ppermute(one, "chip", ring[1])
    three = lax.ppermute(three, "chip", ring[3])
    weights = (here, one, two, three)
    theirs = call(
        functools.partial(gate_up_body, False),
        jax.ShapeDtypeStruct((half, 2 * share), bf16),
        place,
        received,
        *weights,
        scalars=1,
    )
    theirs = lax.ppermute(theirs, "core", swap)
    mine = call(
        functools.partial(gate_up_body, True),
        jax.ShapeDtypeStruct((half, 2 * share), jnp.float32),
        place,
        received,
        *weights,
        scalars=1,
    )
    hidden = call(hidden_body, jax.ShapeDtypeStruct((half * share // 128, 128), bf16), mine, theirs)
    own = lax.all_gather(hidden, "chip", axis=0)
    other = lax.ppermute(own, "core", swap)
    spread = jax.ShapeDtypeStruct((slots, tok_count), bf16)
    down_own, high, low = call(
        down_own_body,
        (jax.ShapeDtypeStruct((half, cols), bf16), spread, spread),
        own,
        w_down[0],
        target_t,
        route_weight.T,
    )
    produced = call(
        down_body,
        jax.ShapeDtypeStruct((experts, cap, cols // 128, 128), bf16),
        place,
        down_own,
        other,
        w_down[0],
        scalars=1,
    )
    returned = lax.all_to_all(produced, ("side", "plane"), split_axis=0, concat_axis=0, tiled=True)
    return call(combine_body, jax.ShapeDtypeStruct((tok_count, cols), bf16), high, low, returned)


def solution(mesh):
    fine = Mesh(
        mesh.devices.reshape(2, mesh.shape["wide"] // 2, CHIPS, 2), ("side", "plane", "chip", "core")
    )
    wide, narrow = ("side", "plane"), ("chip", "core")
    return jax.shard_map(
        on_device,
        mesh=fine,
        in_specs=(
            P(wide, None),
            P(wide, None),
            P(wide, None),
            P(wide, None, narrow),
            P(wide, None, narrow),
            P(wide, None, narrow),
        ),
        out_specs=P(wide, narrow),
        check_vma=False,
    )
```
